32 devices in a mesh: groups: 2 (over x), tm: 4 (over y, core), tile: 4 (over z).
Axes of the slice: x: 2, y: 2, z: 4, core: 2. Of those that a mesh axis runs over, the one named last changes fastest.
Arguments:
- activations: float32 [24, 8, 64, 384], P(('groups', 'tm'), 'tile'), parts along dimension 0, may hold values from -200 to 200, as said below
- gain_attention: float32 [384], replicated, may hold values from 0.1 to 1.9
- w_query: float32 [384, 384], replicated, may hold values from -10 to 10, as said below
- w_key: float32 [384, 384], replicated, may hold values from -10 to 10, as said below
- w_value: float32 [384, 384], replicated, may hold values from -0.3125 to 0.3125
- w_out: float32 [384, 384], replicated, may hold values from -0.3125 to 0.3125
- gain_conv: float32 [384], replicated, may hold values from 0.1 to 1.9
- conv_weight: float32 [27, 384, 384], P(None, 'tm'), may hold values from -0.0625 to 0.0625
Outputs:
- attended: float32 [24, 8, 64, 384], P(('groups', 'tm'), 'tile'), parts along dimension 0
- conv_out: float32 [24, 8, 64, 384], P(('groups', 'tm'), 'tile'), parts along dimension 0
The draws below stay inside these ranges and needn't reach their ends.
There are 2 independent parts, one for each index of `groups`. The reference program is written for one: setup_inputs(seed, part) draws one part's arguments, and reference() takes and returns one part's arrays. A program takes and returns all parts, laid end to end along the dimension named above; an argument that names none is the same for every part. Nothing has to cross between parts.
Inputs may be any that keep to these rules, and one draw needn't show every extreme that they name: `activations`: finite latent features. `w_query`: finite projection entries. `w_key`: finite projection entries.
All inputs are finite; a program needn't handle non-finite values.
Results may differ from the reference program's by a relative error of at most 0.00023.
Values sent between devices are 32-bit elements; how exact they have to be, the bound alone decides.
A program may use at most 128 MiB of HBM per device.

```python
import math
import jax
import jax.numpy as jnp
from jax import lax

C = 384
W = 64
FRAMES = 12
HEIGHT = 8


def draw_activations(key, part):
    base_key = jax.random.fold_in(key, 101)
    row_key = jax.random.fold_in(key, 102)
    column_key = jax.random.fold_in(key, 103)
    shape = (FRAMES, HEIGHT, W, C)
    row_scale = jnp.exp(jax.random.uniform(row_key, (FRAMES, HEIGHT, W, 1), jnp.float32, 0.0, math.log(10.0)))
    column_scale = jnp.exp(jax.random.uniform(column_key, (C,), jnp.float32, 0.0, math.log(10.0)))
    base = jnp.clip(jax.random.normal(base_key, shape, jnp.float32), -6.0, 6.0)
    values = base * row_scale * column_scale / 10.0
    return values.astype(jnp.float32)


def draw_w_query(key, part):
    base = jnp.clip(jax.random.normal(jax.random.fold_in(key, 201), (C, C), jnp.float32), -6.0, 6.0)
    return (2.5 * base / math.sqrt(C)).astype(jnp.float32)


def draw_w_key(key, part):
    base = jnp.clip(jax.random.normal(jax.random.fold_in(key, 203), (C, C), jnp.float32), -6.0, 6.0)
    return (base / math.sqrt(C)).astype(jnp.float32)


def block_scale(rng, shape, split, low, top_value):
    level, own = 1.0, jax.random.fold_in(rng, 6)
    for dim, blocks in split:
        heights = jnp.exp(jax.random.uniform(jax.random.fold_in(own, dim), (blocks,), jnp.float32, low / len(split), top_value / len(split)))
        level = level * jnp.repeat(heights, shape[dim] // blocks).reshape([-1 if axis == dim else 1 for axis in range(len(shape))])
    return level


def gaussian(rng, shape, width, bound, pieces=(), kind=jnp.bfloat16):
    level = block_scale(rng, shape, pieces, -0.22, 0.18) if pieces else 1.0
    drawn = jax.random.normal(rng, shape, jnp.float32) * width * level
    return jnp.minimum(jnp.maximum(drawn, -bound), bound).astype(kind)


def setup_inputs(seed: int = 0, part: int = 0) -> dict:
    keys = jax.random.split(jax.random.key(seed), 9)
    own_keys = jax.random.split(jax.random.fold_in(keys[8], part), 9)
    activations = draw_activations(jax.random.fold_in(jax.random.fold_in(keys[8], part), 71), part)
    gain_attention = jnp.clip(1.0 + 0.18 * jax.random.normal(keys[1], (C,), jnp.float32), 0.1, 1.9)
    w_query = draw_w_query(jax.random.fold_in(keys[8], 71), part)
    w_key = draw_w_key(jax.random.fold_in(keys[8], 71), part)
    w_value = gaussian(keys[4], (C, C), C ** -0.5, 0.3125, (), jnp.float32)
    w_out = gaussian(keys[5], (C, C), C ** -0.5, 0.3125, (), jnp.float32)
    gain_conv = jnp.clip(1.0 + 0.18 * jax.random.normal(keys[6], (C,), jnp.float32), 0.1, 1.9)
    conv_weight = gaussian(keys[7], (27, C, C), (27 * C) ** -0.5, 0.0625, ((1, 4),), jnp.float32)
    return dict(activations=activations, gain_attention=gain_attention, w_query=w_query, w_key=w_key, w_value=w_value, w_out=w_out, gain_conv=gain_conv, conv_weight=conv_weight)


def rms_scale(values, gain):
    return values * lax.rsqrt(lax.optimization_barrier(jnp.mean(values * values, axis=-1, keepdims=True)) + 1e-06) * gain

def reference(activations, gain_attention, w_query, w_key, w_value, w_out, gain_conv, conv_weight):
    highest = lax.Precision.HIGHEST
    frame_count, height_cells, width_cells, channels = activations.shape
    normed = rms_scale(activations, gain_attention).reshape(frame_count, height_cells * width_cells, channels)
    queries = jnp.einsum('fpc,cd->fpd', normed, w_query, precision=highest)
    key_rows = jnp.einsum('fpc,cd->fpd', normed, w_key, precision=highest)
    values = jnp.einsum('fpc,cd->fpd', normed, w_value, precision=highest)
    scale = 1.0 / jnp.sqrt(jnp.float32(channels))

    def one_frame(triple):
        query_frame, key_frame, value_frame = triple
        scores = jnp.dot(query_frame, key_frame.T, precision=highest) * scale
        weights = jax.nn.softmax(scores, axis=-1)
        return jnp.dot(weights, value_frame, precision=highest)
    mixed = lax.map(one_frame, (queries, key_rows, values))
    attended = activations + jnp.einsum('fpc,cd->fpd', mixed, w_out, precision=highest).reshape(activations.shape)
    hidden = jax.nn.silu(rms_scale(attended, gain_conv))
    padded = jnp.pad(hidden, ((2, 0), (1, 1), (1, 1), (0, 0)))
    conv_out = jnp.zeros(activations.shape, jnp.float32)
    for shift_t in range(3):
        for shift_y in range(3):
            for shift_x in range(3):
                window = padded[shift_t:shift_t + frame_count, shift_y:shift_y + height_cells, shift_x:shift_x + width_cells]
                conv_out = conv_out + jnp.einsum('thwc,cd->thwd', window, conv_weight[9 * shift_t + 3 * shift_y + shift_x], precision=highest)
    return (attended, conv_out)
```

```python
import functools
import math

import jax
import jax.numpy as jnp
from jax import lax
from jax.experimental import pallas as pl
from jax.experimental.pallas import tpu as pltpu
from jax.sharding import PartitionSpec as P

F32, BF16 = jnp.float32, jnp.bfloat16
VMEM_LIMIT = 56 * 1024 * 1024
CHUNKS = 3


def split(x):
    high = x.astype(BF16)
    return high, (x - high.astype(F32)).astype(BF16)


def dot3(a, b, dims=(((1,), (0,)), ((), ()))):
    dot = functools.partial(lax.dot_general, dimension_numbers=dims, preferred_element_type=F32)
    (ah, al), (bh, bl) = a, b
    return dot(ah, bh) + (dot(ah, bl) + dot(al, bh))


TRANSPOSED = (((1,), (1,)), ((), ()))


def rms(v, gain):
    return v * lax.rsqrt(jnp.mean(v * v, axis=-1, keepdims=True) + 1e-06) * gain


MESH = pl.DeviceIdType.MESH


def shard_plan(shards, halved):
    plan, held = [], [(0, 0, None)]
    bit = 1
    while 2 * bit < shards:
        bit *= 2
    while bit >= 1 and shards > 1:
        arrived = []
        for mask, part, source in held:
            if halved and bit > 1 and part == 0:
                plan.append(("tm", bit, mask, 1, source))
                plan.append(("groups", 1, mask ^ bit, 1, len(plan) - 1))
                arrived += [(mask ^ bit, 1, len(plan) - 2), (mask ^ bit, 2, len(plan) - 1)]
            else:
                plan.append(("tm", bit, mask, part, source))
                arrived.append((mask ^ bit, part, len(plan) - 1))
        held += arrived
        bit //= 2
    return plan


def kernel(
    plan, times, tiles, act, gain_a, wq, wk, wv, wo, gain_c, kernel_hbm, attended, out,
    others, hid, up, down, past, past_up, past_down, weights, xh, xl,
    line_send, line_recv, edge_send, edge_recv, shard_send, shard_recv, own_sem,
):
    frames, rows, width, channels = hid.shape
    tokens = rows * width
    group, me, tile = lax.axis_index("groups"), lax.axis_index("tm"), lax.axis_index("tile")
    size = kernel_hbm.shape[1]
    half = size // 2

    barrier = pltpu.get_barrier_semaphore()
    friends = [(True, {"groups": 1 - group})]
    bit = 1
    while bit < times:
        friends.append((True, {"tm": me + bit * (1 - 2 * ((me // bit) % 2))}))
        bit *= 2
    for dt, dz in ((0, 1), (1, 0), (1, 1), (1, -1)):
        for sign in (1, -1):
            t, z = me + sign * dt, tile + sign * dz
            inside = (t >= 0) & (t < times) & (z >= 0) & (z < tiles)
            friends.append((inside, {"tm": t, "tile": z}))
    count = 0
    for inside, device in friends:
        if inside is True:
            pl.semaphore_signal(barrier, inc=1, device_id=device, device_id_type=MESH)
            count = count + 1
        else:

            @pl.when(inside)
            def _(device=device):
                pl.semaphore_signal(barrier, inc=1, device_id=device, device_id_type=MESH)

            count = count + inside.astype(jnp.int32)
    pl.semaphore_wait(barrier, count)

    def copy(src, dst, send, recv, device):
        return pltpu.make_async_remote_copy(
            src_ref=src, dst_ref=dst, send_sem=send, recv_sem=recv, device_id=device, device_id_type=MESH
        )

    def line(f, distance, direction):
        slot_here = distance - 1 if direction > 0 else tiles - distance + 1
        slot_there = distance if direction > 0 else tiles - distance
        src = act.at[f] if distance == 1 else others.at[f, slot_here - 1]
        side = 0 if direction > 0 else 1
        return copy(
            src, others.at[f, slot_there - 1], line_send.at[f, side, distance - 1],
            line_recv.at[f, slot_there - 1], {"tile": tile + direction},
        )

    def sends(distance, direction):
        if direction > 0:
            return (tile >= distance - 1) & (tile < tiles - 1)
        return (tile + distance - 1 <= tiles - 1) & (tile > 0)

    def flip(value, bit):
        return value + bit * (1 - 2 * ((value // bit) % 2))

    def flipped(mask):
        value, bit = me, 1
        while bit <= mask:
            if mask & bit:
                value = flip(value, bit)
            bit *= 2
        return value

    def region(ref, chunk, shard, part, swap, local=False):
        first = group if not swap else 1 - group
        start = {0: 0, 1: first * half, 2: (1 - first) * half}[part]
        row = start if local else shard * size + start
        length = size if part == 0 else half
        if not isinstance(row, int):
            row = pl.multiple_of(row, math.gcd(size, length))
        return ref.at[pl.ds(9 * chunk, 9), pl.ds(row, length)]

    def shard_copy(chunk, k):
        axis, bit, mask, part, source = plan[k]
        there = region(weights, chunk, flipped(mask), part, False)
        src = region(kernel_hbm, chunk, 0, part, False, True) if mask == 0 else there
        device = {"tm": flip(me, bit)} if axis == "tm" else {"groups": 1 - group}
        return copy(src, there, shard_send.at[chunk, k], shard_recv.at[chunk, k], device)

    def shard_arrival(chunk, k):
        axis, bit, mask, part, source = plan[k]
        if axis == "tm":
            here, device = region(weights, chunk, flipped(mask ^ bit), part, False), {"tm": flip(me, bit)}
        else:
            here, device = region(weights, chunk, flipped(mask), part, True), {"groups": 1 - group}
        return copy(here, here, shard_send.at[chunk, k], shard_recv.at[chunk, k], device)

    early = [k for k, step in enumerate(plan) if step[4] is None and any(s[4] == k for s in plan)]
    later = [k for k, step in enumerate(plan) if step[4] is not None and any(s[4] == k for s in plan)]

    waited = set()

    def arrive(chunk, k):
        if (chunk, k) in waited:
            return
        waited.add((chunk, k))
        shard_arrival(chunk, k).wait_recv()
        if k in early and chunk + 1 < CHUNKS:
            shard_copy(chunk + 1, k).start()
        for j, step in enumerate(plan):
            if step[4] == k:
                shard_copy(chunk, j).start()

    def start_line(f):
        for direction in (1, -1):

            @pl.when(sends(1, direction))
            def _(direction=direction):
                line(f, 1, direction).start()

    start_line(0)
    for chunk in range(CHUNKS):
        for k, step in enumerate(plan):
            if step[4] is None and (chunk == 0 or k not in early):
                shard_copy(chunk, k).start()
    own_rows = weights.at[:, pl.ds(pl.multiple_of(me * size, size), size)]
    own_copy = pltpu.make_async_copy(kernel_hbm, own_rows, own_sem)
    own_copy.start()

    cell = lax.broadcasted_iota(jnp.int32, (width, channels), 0)

    def place(f, r):
        upper, middle, lower, t = (past_up, past, past_down, f) if f < 2 else (up, hid, down, f - 2)
        value = upper[t] if r == 0 else lower[t] if r == rows + 1 else middle[t, r - 1]
        before = jnp.where(cell == 0, 0.0, pltpu.roll(value, 1, 0))
        after = jnp.where(cell == width - 1, 0.0, pltpu.roll(value, width - 1, 0))
        for c, v in enumerate((before, value, after)):
            high, low = split(v)
            xh[f, r, :, c * channels : (c + 1) * channels] = high
            xl[f, r, :, c * channels : (c + 1) * channels] = low

    gain = gain_a[...].reshape(1, channels)
    scale = 1.0 / math.sqrt(channels)
    edges = []

    def edge(number, src, dst, dt, dz):
        t, z = me + dt, tile + dz
        goes = (t < times) & (z >= 0) & (z < tiles)
        comes = (me - dt >= 0) & (tile - dz >= 0) & (tile - dz < tiles)
        move = copy(src, dst, edge_send.at[number], edge_recv.at[number], {"tm": t, "tile": z})

        @pl.when(goes)
        def _():
            move.start()

        edges.append((goes, comes, move, dst))

    for f in range(frames):
        for distance in range(1, tiles):
            for direction in (1, -1):
                comes = tile >= distance if direction > 0 else tile + distance < tiles

                @pl.when(comes)
                def _(f=f, distance=distance, direction=direction):
                    slot = distance if direction > 0 else tiles - distance
                    here = others.at[f, slot - 1]
                    side = 0 if direction > 0 else 1
                    copy(
                        here, here, line_send.at[f, side, distance - 1], line_recv.at[f, slot - 1],
                        {"tile": tile - direction},
                    ).wait_recv()

                if distance + 1 < tiles:

                    @pl.when(sends(distance + 1, direction))
                    def _(f=f, distance=distance, direction=direction):
                        line(f, distance + 1, direction).start()

            if distance == 1 and f + 1 < frames:
                start_line(f + 1)
        if tiles == 1 and f + 1 < frames:
            start_line(f + 1)
        if f < CHUNKS and f < frames - 1:
            for k in early:
                arrive(f, k)
        x = act[f]
        normed = split(rms(x, gain))
        queries = dot3(normed, split(wq[...]))
        folded = split(dot3(split(queries), split(wk[...]), TRANSPOSED))
        cells = [normed] + [split(rms(others[f, s], gain)) for s in range(tiles - 1)]
        keys = tuple(jnp.concatenate([c[i] for c in cells], axis=0) for i in range(2))
        scores = dot3(folded, keys, TRANSPOSED) * scale
        powers = jnp.exp(scores - jnp.max(scores, axis=-1, keepdims=True))
        summed = jnp.sum(powers, axis=-1, keepdims=True)
        gathered = dot3(split(powers), keys) / summed
        mixed = dot3(split(gathered), split(wv[...]))
        result = x + dot3(split(mixed), split(wo[...]))
        attended[f] = result
        v = rms(result, gain_c[...].reshape(1, channels))
        hid[f] = (v / (1.0 + jnp.exp(-v))).reshape(rows, width, channels)
        base = 5 * f
        edge(base, hid.at[f, rows - 1], up.at[f], 0, 1)
        edge(base + 1, hid.at[f, 0], down.at[f], 0, -1)
        if f >= frames - 2:
            p = f - (frames - 2)
            edge(base + 2, hid.at[f], past.at[p], 1, 0)
            edge(base + 3, hid.at[f, rows - 1], past_up.at[p], 1, 1)
            edge(base + 4, hid.at[f, 0], past_down.at[p], 1, -1)
        for r in range(1, rows + 1):
            place(f + 2, r)
        if 1 <= f < frames - 1 and f <= CHUNKS:
            for k in later:
                arrive(f - 1, k)

    for chunk in range(CHUNKS):
        for k in early:
            arrive(chunk, k)
    for goes, comes, move, dst in edges:

        @pl.when(comes)
        def _(move=move):
            move.wait_recv()

        @pl.when(jnp.logical_not(comes))
        def _(dst=dst):
            dst[...] = jnp.zeros(dst.shape, F32)

    for f in range(frames + 2):
        for r in range(rows + 2):
            if f < 2 or r in (0, rows + 1):
                place(f, r)
    for chunk in range(CHUNKS):
        for k in later:
            arrive(chunk, k)
    own_copy.wait()
    pixels = frames * tokens
    for a in range(CHUNKS):
        for k in range(len(plan)):
            arrive(a, k)

        def row_taps(b, carry, a=a):
            block = weights[pl.ds(9 * a + 3 * b, 3)].reshape(3 * channels, channels)
            high = xh[pl.ds(a, frames), pl.ds(b, rows)].reshape(pixels, 3 * channels)
            low = xl[pl.ds(a, frames), pl.ds(b, rows)].reshape(pixels, 3 * channels)
            product = dot3((high, low), split(block))
            out[...] = out[...] + product
            return carry

        if a == 0:
            out[...] = jnp.zeros(out.shape, F32)
        lax.fori_loop(0, 3, row_taps, 0)

    for f in range(frames):
        for distance in range(1, tiles):
            for direction in (1, -1):

                @pl.when(sends(distance, direction))
                def _(f=f, distance=distance, direction=direction):
                    line(f, distance, direction).wait_send()

    for goes, comes, move, dst in edges:

        @pl.when(goes)
        def _(move=move):
            move.wait_send()

    for chunk in range(CHUNKS):
        for k in range(len(plan)):
            shard_copy(chunk, k).wait_send()


BLOCKS = 9
QUARTERED = ()


def pair_kernel(
    act_hbm, gain_a_hbm, wq_hbm, wk_hbm, wv_hbm, wo_hbm, gain_c_hbm, kernel_hbm, attended, out,
    act, gain_a, wq, wk, wv, wo, gain_c, others, hid, ret, ret_in, weights, m1h, m1l, m2h, m2l, xh, xl,
    local_sem, line_send, line_recv, ret_send, ret_recv, past_send, past_recv, shard_send, shard_recv, core_send, core_recv,
):
    frames, tokens, channels = act.shape
    width = hid.shape[2]
    rows = tokens // width
    group, me, tile = lax.axis_index("groups"), lax.axis_index("tm"), lax.axis_index("tile")
    size = kernel_hbm.shape[1]
    half, quarter = size // 2, size // 4
    inner = (tile == 1) | (tile == 2)
    outer = jnp.logical_not(inner)
    low = tile < 2
    place_in_pair = inner.astype(jnp.int32)
    core_of = me % 2
    side = (me // 2) % 2
    x_partner = {"groups": 1 - group}
    y_partner = {"tm": me + 2 - 4 * side}
    core_partner = {"tm": me + 1 - 2 * core_of}
    pair_partner = {"tile": tile + 1 - 2 * (tile % 2)}
    peer = {"tile": 3 - tile}
    later = {"tm": me + 1}
    sends_past, has_past = me < 3, me > 0

    locals_in = [(act_hbm, act), (gain_a_hbm, gain_a), (wq_hbm, wq), (wk_hbm, wk), (wv_hbm, wv), (wo_hbm, wo), (gain_c_hbm, gain_c)]
    local = [pltpu.make_async_copy(src, dst, local_sem.at[i]) for i, (src, dst) in enumerate(locals_in)]
    own_rows = weights.at[:, pl.ds(pl.multiple_of(me * size, size), size)]
    local.append(pltpu.make_async_copy(kernel_hbm, own_rows, local_sem.at[len(locals_in)]))
    for c in local:
        c.start()

    barrier = pltpu.get_barrier_semaphore()

    def greet(device):
        pl.semaphore_signal(barrier, inc=1, device_id=device, device_id_type=MESH)

    for device in (x_partner, y_partner, core_partner, pair_partner):
        greet(device)
    pl.when(inner)(lambda: greet(peer))
    crossing = me == 1, me == 2
    pl.when(crossing[0])(lambda: greet({"tm": me + 1}))
    pl.when(crossing[1])(lambda: greet({"tm": me - 1}))
    pl.semaphore_wait(barrier, 4 + inner.astype(jnp.int32) + (crossing[0] | crossing[1]).astype(jnp.int32))

    def copy(src, dst, send, recv, device):
        return pltpu.make_async_remote_copy(
            src_ref=src, dst_ref=dst, send_sem=send, recv_sem=recv, device_id=device, device_id_type=MESH
        )

    def line(f, slot):
        src = others.at[f, 0] if slot == 2 else act_hbm.at[f]
        return copy(src, others.at[f, slot], line_send.at[f, slot], line_recv.at[f, slot], pair_partner if slot == 0 else peer)

    def back(f, part):
        if part == 0:
            return copy(ret.at[f], ret_in.at[f], ret_send.at[f, 0], ret_recv.at[f, 0], pair_partner)
        near, far = jnp.where(low, 1, rows), jnp.where(low, rows + 1, 0)
        return copy(hid.at[f + 2, near], hid.at[f + 2, far], ret_send.at[f, 1], ret_recv.at[f, 1], pair_partner)

    def back_arrival(f, part):
        if part == 0:
            return copy(ret_in.at[f], ret_in.at[f], ret_send.at[f, 0], ret_recv.at[f, 0], pair_partner)
        here = hid.at[f + 2, jnp.where(low, rows + 1, 0)]
        return copy(here, here, ret_send.at[f, 1], ret_recv.at[f, 1], pair_partner)

    def past(f):
        return copy(hid.at[f + 2], hid.at[f - 1], past_send.at[f - 1], past_recv.at[f - 1], later)

    def past_arrival(f):
        return copy(hid.at[f - 1], hid.at[f - 1], past_send.at[f - 1], past_recv.at[f - 1], later)

    def taps_of(k):
        return pl.ds(9 * (2 - k // 3) + 3 * (k % 3), 3)

    def region(ref, k, shard, which, where):
        row = which * half
        length = half
        if where is not None:
            row, length = row + where * quarter, quarter
        if shard is not None:
            row = row + shard * size
        return ref.at[taps_of(k), pl.ds(pl.multiple_of(row, quarter), length)]

    foreign, theirs = me + 2 - 4 * side, me + 1 - 2 * core_of
    there = theirs + 2 - 4 * side

    def shard_copy(kind, k):
        q = place_in_pair if k in QUARTERED else None
        sems = shard_send.at[kind, k], shard_recv.at[kind, k]
        if kind == 0:
            return copy(region(kernel_hbm, k, None, group, q), region(weights, k, me, group, q), *sems, y_partner)
        if kind == 1:
            ref = region(weights, k, foreign, group, q)
            return copy(ref, ref, *sems, x_partner)
        if kind in (2, 3):
            ref = region(weights, k, foreign, group if kind == 2 else 1 - group, None)
            return copy(ref, ref, *sems, core_partner)
        ref = region(weights, k, foreign, group if kind == 4 else 1 - group, q)
        return copy(ref, ref, *sems, pair_partner)

    def shard_arrival(kind, k):
        q = place_in_pair if k in QUARTERED else None
        sems = shard_send.at[kind, k], shard_recv.at[kind, k]
        if kind == 0:
            ref, device = region(weights, k, foreign, group, q), y_partner
        elif kind == 1:
            ref, device = region(weights, k, foreign, 1 - group, q), x_partner
        elif kind in (2, 3):
            ref, device = region(weights, k, there, group if kind == 2 else 1 - group, None), core_partner
        else:
            ref, device = region(weights, k, foreign, group if kind == 4 else 1 - group, 1 - q), pair_partner
        return copy(ref, ref, *sems, device)

    started = []

    def send(kind, k):
        started.append((kind, k))
        shard_copy(kind, k).start()

    done = set()

    def step(k, stage):
        if k < 0 or (k, stage) in done:
            return
        done.add((k, stage))
        quartered = k in QUARTERED
        if stage == 0:
            shard_arrival(0, k).wait_recv()
            if k + 2 < BLOCKS:
                send(0, k + 2)
            send(1, k)
            send(4 if quartered else 2, k)
        elif stage == 1:
            shard_arrival(1, k).wait_recv()
            if quartered:
                send(5, k)
                shard_arrival(4, k).wait_recv()
                send(2, k)
            else:
                send(3, k)
        elif quartered:
            shard_arrival(5, k).wait_recv()
            send(3, k)

    def service(k):
        step(k, 0)
        step(k - 1, 1)
        step(k - 2, 2)

    core_copies = [
        copy(
            kernel_hbm.at[pl.ds(9 * a, 9)], weights.at[pl.ds(9 * a, 9), pl.ds(pl.multiple_of(me * size, size), size)],
            core_send.at[a], core_recv.at[a], core_partner,
        )
        for a in (2, 1, 0)
    ]

    def core_arrival(a):
        ref = weights.at[pl.ds(9 * a, 9), pl.ds(pl.multiple_of(theirs * size, size), size)]
        return copy(ref, ref, core_send.at[a], core_recv.at[a], core_partner)

    @pl.when(inner)
    def _():
        line(0, 1).start()

    @pl.when(outer)
    def _():
        line(0, 0).start()

    send(0, 0)
    send(0, 1)
    for c in core_copies:
        c.start()

    for c in local[:-1]:
        c.wait()
    gain = gain_a[...].reshape(1, channels)
    gain_2 = gain_c[...].reshape(1, channels)

    @pl.when(outer)
    def _():
        line(0, 0).wait_send()
        line(1, 0).start()

    @pl.when(inner)
    def _():
        m1 = dot3(split(wq[...]), split(wk[...]), TRANSPOSED) * (1.0 / math.sqrt(channels))
        m1h[...], m1l[...] = split(m1)
        m2h[...], m2l[...] = split(dot3(split(wv[...]), split(wo[...])))
        line(0, 0).wait_recv()
        line(0, 2).start()

    cell = lax.broadcasted_iota(jnp.int32, (width, channels), 0)

    def place(t, r):
        value = hid[t, r]
        before = jnp.where(cell == 0, 0.0, pltpu.roll(value, 1, 0))
        after = jnp.where(cell == width - 1, 0.0, pltpu.roll(value, width - 1, 0))
        for c, v in enumerate((before, value, after)):
            xh[t, r, :, c * channels : (c + 1) * channels], xl[t, r, :, c * channels : (c + 1) * channels] = split(v)

    def activate(v):
        v = rms(v, gain_2)
        return v / (1.0 + jnp.exp(-v))

    def attend(f):
        own, far_out = act[f], others[f, 0]
        beside = others[f, 1, pl.ds(pl.multiple_of(jnp.where(low, 0, tokens - width), width), width)]
        cells = [split(rms(v, gain)) for v in (own, far_out, others[f, 1], others[f, 2])]
        keys = tuple(jnp.concatenate([c[i] for c in cells], axis=0) for i in range(2))
        asked = jnp.concatenate([own, far_out, beside], axis=0)
        near = split(rms(beside, gain))
        normed = tuple(jnp.concatenate([cells[0][i], cells[1][i], near[i]], axis=0) for i in range(2))
        folded = split(dot3(normed, (m1h[...], m1l[...])))
        scores = dot3(folded, keys, TRANSPOSED)
        powers = jnp.exp(scores - jnp.max(scores, axis=-1, keepdims=True))
        summed = jnp.sum(powers, axis=-1, keepdims=True)
        gathered = dot3(split(powers), keys) / summed
        result = asked + dot3(split(gathered), (m2h[...], m2l[...]))
        ret[f] = result[tokens : 2 * tokens]
        back(f, 0).start()
        hidden = activate(result)
        hid[f + 2, 1 : rows + 1] = hidden[:tokens].reshape(rows, width, channels)
        back(f, 1).start()
        attended[f] = result[:tokens]
        edge = jnp.where(low, hidden[2 * tokens - width : 2 * tokens], hidden[tokens : tokens + width])
        beyond = hidden[2 * tokens :]
        hid[f + 2, 0] = jnp.where(low, edge, beyond)
        hid[f + 2, rows + 1] = jnp.where(low, beyond, edge)

    def settle(f):
        if f > 0:

            @pl.when(sends_past)
            def _():
                past(f).start()

        for r in range(rows + 2):
            place(f + 2, r)

    def receive(f):
        back_arrival(f, 0).wait_recv()
        result = ret_in[f]
        attended[f] = result
        hid[f + 2, 1 : rows + 1] = activate(result).reshape(rows, width, channels)
        hid[f + 2, jnp.where(low, 0, rows + 1)] = jnp.zeros((width, channels), F32)
        back_arrival(f, 1).wait_recv()

    for f in range(frames):

        @pl.when(inner)
        def _():
            line(f, 1).wait_recv()
            if f + 1 < frames:
                line(f + 1, 1).start()

        if f == 0:

            @pl.when(outer)
            def _():
                line(1, 0).wait_send()
                line(2, 0).start()

        service(2 * f)

        @pl.when(inner)
        def _():
            line(f, 2).wait_recv()
            if f + 1 < frames:
                line(f + 1, 0).wait_recv()
                line(f + 1, 2).start()
            attend(f)
            settle(f)

        service(2 * f + 1)
        if f > 0:

            @pl.when(outer)
            def _():
                receive(f - 1)
                settle(f - 1)

    service(6)

    @pl.when(outer)
    def _():
        receive(frames - 1)
        settle(frames - 1)

    local[-1].wait()
    pixels = frames * tokens

    def conv(first, count):
        def row_taps(k, carry):
            a, b = 2 - k // 3, k % 3
            block = weights[taps_of(k)].reshape(3 * channels, channels)
            high = xh[pl.ds(a, frames), pl.ds(b, rows)].reshape(pixels, 3 * channels)
            lo = xl[pl.ds(a, frames), pl.ds(b, rows)].reshape(pixels, 3 * channels)
            out[...] = out[...] + dot3((high, lo), split(block))
            return carry

        lax.fori_loop(first, first + count, row_taps, 0)

    ready_blocks = set()

    def ready(k):
        for stage in range(3):
            step(k, stage)
        for kind in (2, 3):
            shard_arrival(kind, k).wait_recv()
        if k % 3 == 0:
            core_arrival(2 - k // 3).wait_recv()

    out[...] = jnp.zeros(out.shape, F32)
    for first, count, then in ((0, 3, 7), (3, 2, 8), (5, 1, None), (6, 1, None), (7, 1, None), (8, 1, None)):
        if first == 3:

            @pl.when(has_past)
            def _():
                past_arrival(1).wait_recv()
                past_arrival(2).wait_recv()

            @pl.when(jnp.logical_not(has_past))
            def _():
                hid[0:2] = jnp.zeros((2, *hid.shape[1:]), F32)

            for t in range(2):
                for r in range(rows + 2):
                    place(t, r)
        for k in range(first, first + count):
            ready(k)
        conv(first, count)
        if then is not None:
            service(then)

    for f in range(frames):

        @pl.when(inner)
        def _():
            line(f, 1).wait_send()
            line(f, 2).wait_send()
            back(f, 0).wait_send()
            back(f, 1).wait_send()

    @pl.when(outer)
    def _():
        line(2, 0).wait_send()

    @pl.when(sends_past)
    def _():
        past(1).wait_send()
        past(2).wait_send()

    for c in core_copies:
        c.wait_send()
    for kind, k in started:
        shard_copy(kind, k).wait_send()


def paired(own, gain_attention, w_query, w_key, w_value, w_out, gain_conv, conv_weight, rows):
    frames, tokens, channels = own.shape
    width = tokens // rows
    taps = conv_weight.shape[0]
    vmem, dma = pltpu.VMEM, pltpu.SemaphoreType.DMA
    return pl.pallas_call(
        pair_kernel,
        in_specs=[pl.BlockSpec(memory_space=pl.ANY)] * 8,
        out_specs=[pl.BlockSpec(memory_space=pltpu.VMEM)] * 2,
        out_shape=[
            jax.ShapeDtypeStruct(own.shape, F32),
            jax.ShapeDtypeStruct((frames * tokens, channels), F32),
        ],
        scratch_shapes=[
            vmem(own.shape, F32),
            vmem((channels,), F32),
            *[vmem((channels, channels), F32)] * 4,
            vmem((channels,), F32),
            vmem((frames, 3, tokens, channels), F32),
            vmem((frames + 2, rows + 2, width, channels), F32),
            vmem((frames, tokens, channels), F32),
            vmem((frames, tokens, channels), F32),
            vmem((taps, channels, channels), F32),
            *[vmem((channels, channels), BF16)] * 4,
            *[vmem((frames + 2, rows + 2, width, 3 * channels), BF16)] * 2,
            dma((8,)),
            dma((frames, 3)),
            dma((frames, 3)),
            dma((frames, 2)),
            dma((frames, 2)),
            dma((2,)),
            dma((2,)),
            dma((6, BLOCKS)),
            dma((6, BLOCKS)),
            dma((3,)),
            dma((3,)),
        ],
        compiler_params=pltpu.CompilerParams(
            collective_id=0, has_side_effects=True, vmem_limit_bytes=VMEM_LIMIT
        ),
    )(own, gain_attention, w_query, w_key, w_value, w_out, gain_conv, conv_weight)


def body(activations, gain_attention, w_query, w_key, w_value, w_out, gain_conv, conv_weight):
    frames, rows, width, channels = activations.shape
    tokens = rows * width
    own = activations.reshape(frames, tokens, channels)
    times, tiles = lax.axis_size("tm"), lax.axis_size("tile")
    taps, size = conv_weight.shape[:2]
    if (lax.axis_size("groups"), times, tiles) == (2, 4, 4) and (frames, rows, taps) == (3, 2, 27) and size % 32 == 0:
        attended, conv_out = paired(
            own, gain_attention, w_query, w_key, w_value, w_out, gain_conv, conv_weight, rows
        )
        return (attended.reshape(activations.shape), conv_out.reshape(activations.shape))
    plan = shard_plan(times, lax.axis_size("groups") == 2 and size % 16 == 0)
    vmem = pl.BlockSpec(memory_space=pltpu.VMEM)
    dma = pltpu.SemaphoreType.DMA
    attended, conv_out = pl.pallas_call(
        functools.partial(kernel, plan, times, tiles),
        in_specs=[vmem] * 7 + [pl.BlockSpec(memory_space=pl.ANY)],
        out_specs=[vmem, vmem],
        out_shape=[
            jax.ShapeDtypeStruct(own.shape, F32),
            jax.ShapeDtypeStruct((frames * tokens, channels), F32),
        ],
        scratch_shapes=[
            pltpu.VMEM((frames, tiles - 1, tokens, channels), F32),
            pltpu.VMEM((frames, rows, width, channels), F32),
            pltpu.VMEM((frames, width, channels), F32),
            pltpu.VMEM((frames, width, channels), F32),
            pltpu.VMEM((2, rows, width, channels), F32),
            pltpu.VMEM((2, width, channels), F32),
            pltpu.VMEM((2, width, channels), F32),
            pltpu.VMEM((taps, channels, channels), F32),
            pltpu.VMEM((frames + 2, rows + 2, width, 3 * channels), BF16),
            pltpu.VMEM((frames + 2, rows + 2, width, 3 * channels), BF16),
            dma((frames, 2, tiles - 1)),
            dma((frames, tiles - 1)),
            dma((5 * frames,)),
            dma((5 * frames,)),
            dma((CHUNKS, len(plan))),
            dma((CHUNKS, len(plan))),
            dma,
        ],
        compiler_params=pltpu.CompilerParams(
            collective_id=0, has_side_effects=True, vmem_limit_bytes=VMEM_LIMIT
        ),
    )(
        own, gain_attention, w_query, w_key, w_value, w_out, gain_conv, conv_weight
    )
    return (attended.reshape(activations.shape), conv_out.reshape(activations.shape))


def solution(mesh):
    placed = P(("groups", "tm"), "tile", None, None)
    return jax.shard_map(
        body,
        mesh=mesh,
        in_specs=(placed, P(), P(), P(), P(), P(), P(), P(None, "tm", None)),
        out_specs=(placed, placed),
        check_vma=False,
    )
```

```python
import functools
import math

import jax
import jax.numpy as jnp
from jax import lax
from jax.experimental import pallas as pl
from jax.experimental.pallas import tpu as pltpu
from jax.sharding import PartitionSpec as P

F32, BF16 = jnp.float32, jnp.bfloat16
VMEM_LIMIT = 56 * 1024 * 1024
CHUNKS = 3


def split(x):
    high = x.astype(BF16)
    return high, (x - high.astype(F32)).astype(BF16)


def dot3(a, b, dims=(((1,), (0,)), ((), ()))):
    dot = functools.partial(lax.dot_general, dimension_numbers=dims, preferred_element_type=F32)
    (ah, al), (bh, bl) = a, b
    return dot(ah, bh) + (dot(ah, bl) + dot(al, bh))


TRANSPOSED = (((1,), (1,)), ((), ()))


def rms(v, gain):
    return v * lax.rsqrt(jnp.mean(v * v, axis=-1, keepdims=True) + 1e-06) * gain


MESH = pl.DeviceIdType.MESH


def shard_plan(shards, halved):
    plan, held = [], [(0, 0, None)]
    bit = 1
    while 2 * bit < shards:
        bit *= 2
    while bit >= 1 and shards > 1:
        arrived = []
        for mask, part, source in held:
            if halved and bit > 1 and part == 0:
                plan.append(("tm", bit, mask, 1, source))
                plan.append(("groups", 1, mask ^ bit, 1, len(plan) - 1))
                arrived += [(mask ^ bit, 1, len(plan) - 2), (mask ^ bit, 2, len(plan) - 1)]
            else:
                plan.append(("tm", bit, mask, part, source))
                arrived.append((mask ^ bit, part, len(plan) - 1))
        held += arrived
        bit //= 2
    return plan


def kernel(
    plan, times, tiles, act, gain_a, wq, wk, wv, wo, gain_c, kernel_hbm, attended, out,
    others, hid, up, down, past, past_up, past_down, weights, xh, xl,
    line_send, line_recv, edge_send, edge_recv, shard_send, shard_recv, own_sem,
):
    frames, rows, width, channels = hid.shape
    tokens = rows * width
    group, me, tile = lax.axis_index("groups"), lax.axis_index("tm"), lax.axis_index("tile")
    size = kernel_hbm.shape[1]
    half = size // 2

    barrier = pltpu.get_barrier_semaphore()
    friends = [(True, {"groups": 1 - group})]
    bit = 1
    while bit < times:
        friends.append((True, {"tm": me + bit * (1 - 2 * ((me // bit) % 2))}))
        bit *= 2
    for dt, dz in ((0, 1), (1, 0), (1, 1), (1, -1)):
        for sign in (1, -1):
            t, z = me + sign * dt, tile + sign * dz
            inside = (t >= 0) & (t < times) & (z >= 0) & (z < tiles)
            friends.append((inside, {"tm": t, "tile": z}))
    count = 0
    for inside, device in friends:
        if inside is True:
            pl.semaphore_signal(barrier, inc=1, device_id=device, device_id_type=MESH)
            count = count + 1
        else:

            @pl.when(inside)
            def _(device=device):
                pl.semaphore_signal(barrier, inc=1, device_id=device, device_id_type=MESH)

            count = count + inside.astype(jnp.int32)
    pl.semaphore_wait(barrier, count)

    def copy(src, dst, send, recv, device):
        return pltpu.make_async_remote_copy(
            src_ref=src, dst_ref=dst, send_sem=send, recv_sem=recv, device_id=device, device_id_type=MESH
        )

    def line(f, distance, direction):
        slot_here = distance - 1 if direction > 0 else tiles - distance + 1
        slot_there = distance if direction > 0 else tiles - distance
        src = act.at[f] if distance == 1 else others.at[f, slot_here - 1]
        side = 0 if direction > 0 else 1
        return copy(
            src, others.at[f, slot_there - 1], line_send.at[f, side, distance - 1],
            line_recv.at[f, slot_there - 1], {"tile": tile + direction},
        )

    def sends(distance, direction):
        if direction > 0:
            return (tile >= distance - 1) & (tile < tiles - 1)
        return (tile + distance - 1 <= tiles - 1) & (tile > 0)

    def flip(value, bit):
        return value + bit * (1 - 2 * ((value // bit) % 2))

    def flipped(mask):
        value, bit = me, 1
        while bit <= mask:
            if mask & bit:
                value = flip(value, bit)
            bit *= 2
        return value

    def region(ref, chunk, shard, part, swap, local=False):
        first = group if not swap else 1 - group
        start = {0: 0, 1: first * half, 2: (1 - first) * half}[part]
        row = start if local else shard * size + start
        length = size if part == 0 else half
        if not isinstance(row, int):
            row = pl.multiple_of(row, math.gcd(size, length))
        return ref.at[pl.ds(9 * chunk, 9), pl.ds(row, length)]

    def shard_copy(chunk, k):
        axis, bit, mask, part, source = plan[k]
        there = region(weights, chunk, flipped(mask), part, False)
        src = region(kernel_hbm, chunk, 0, part, False, True) if mask == 0 else there
        device = {"tm": flip(me, bit)} if axis == "tm" else {"groups": 1 - group}
        return copy(src, there, shard_send.at[chunk, k], shard_recv.at[chunk, k], device)

    def shard_arrival(chunk, k):
        axis, bit, mask, part, source = plan[k]
        if axis == "tm":
            here, device = region(weights, chunk, flipped(mask ^ bit), part, False), {"tm": flip(me, bit)}
        else:
            here, device = region(weights, chunk, flipped(mask), part, True), {"groups": 1 - group}
        return copy(here, here, shard_send.at[chunk, k], shard_recv.at[chunk, k], device)

    early = [k for k, step in enumerate(plan) if step[4] is None and any(s[4] == k for s in plan)]
    later = [k for k, step in enumerate(plan) if step[4] is not None and any(s[4] == k for s in plan)]

    waited = set()

    def arrive(chunk, k):
        if (chunk, k) in waited:
            return
        waited.add((chunk, k))
        shard_arrival(chunk, k).wait_recv()
        if k in early and chunk + 1 < CHUNKS:
            shard_copy(chunk + 1, k).start()
        for j, step in enumerate(plan):
            if step[4] == k:
                shard_copy(chunk, j).start()

    def start_line(f):
        for direction in (1, -1):

            @pl.when(sends(1, direction))
            def _(direction=direction):
                line(f, 1, direction).start()

    start_line(0)
    for chunk in range(CHUNKS):
        for k, step in enumerate(plan):
            if step[4] is None and (chunk == 0 or k not in early):
                shard_copy(chunk, k).start()
    own_rows = weights.at[:, pl.ds(pl.multiple_of(me * size, size), size)]
    own_copy = pltpu.make_async_copy(kernel_hbm, own_rows, own_sem)
    own_copy.start()

    cell = lax.broadcasted_iota(jnp.int32, (width, channels), 0)

    def place(f, r):
        upper, middle, lower, t = (past_up, past, past_down, f) if f < 2 else (up, hid, down, f - 2)
        value = upper[t] if r == 0 else lower[t] if r == rows + 1 else middle[t, r - 1]
        before = jnp.where(cell == 0, 0.0, pltpu.roll(value, 1, 0))
        after = jnp.where(cell == width - 1, 0.0, pltpu.roll(value, width - 1, 0))
        for c, v in enumerate((before, value, after)):
            high, low = split(v)
            xh[f, r, :, c * channels : (c + 1) * channels] = high
            xl[f, r, :, c * channels : (c + 1) * channels] = low

    gain = gain_a[...].reshape(1, channels)
    scale = 1.0 / math.sqrt(channels)
    edges = []

    def edge(number, src, dst, dt, dz):
        t, z = me + dt, tile + dz
        goes = (t < times) & (z >= 0) & (z < tiles)
        comes = (me - dt >= 0) & (tile - dz >= 0) & (tile - dz < tiles)
        move = copy(src, dst, edge_send.at[number], edge_recv.at[number], {"tm": t, "tile": z})

        @pl.when(goes)
        def _():
            move.start()

        edges.append((goes, comes, move, dst))

    for f in range(frames):
        for distance in range(1, tiles):
            for direction in (1, -1):
                comes = tile >= distance if direction > 0 else tile + distance < tiles

                @pl.when(comes)
                def _(f=f, distance=distance, direction=direction):
                    slot = distance if direction > 0 else tiles - distance
                    here = others.at[f, slot - 1]
                    side = 0 if direction > 0 else 1
                    copy(
                        here, here, line_send.at[f, side, distance - 1], line_recv.at[f, slot - 1],
                        {"tile": tile - direction},
                    ).wait_recv()

                if distance + 1 < tiles:

                    @pl.when(sends(distance + 1, direction))
                    def _(f=f, distance=distance, direction=direction):
                        line(f, distance + 1, direction).start()

            if distance == 1 and f + 1 < frames:
                start_line(f + 1)
        if tiles == 1 and f + 1 < frames:
            start_line(f + 1)
        if f < CHUNKS and f < frames - 1:
            for k in early:
                arrive(f, k)
        x = act[f]
        normed = split(rms(x, gain))
        queries = dot3(normed, split(wq[...]))
        folded = split(dot3(split(queries), split(wk[...]), TRANSPOSED))
        cells = [normed] + [split(rms(others[f, s], gain)) for s in range(tiles - 1)]
        keys = tuple(jnp.concatenate([c[i] for c in cells], axis=0) for i in range(2))
        scores = dot3(folded, keys, TRANSPOSED) * scale
        powers = jnp.exp(scores - jnp.max(scores, axis=-1, keepdims=True))
        summed = jnp.sum(powers, axis=-1, keepdims=True)
        gathered = dot3(split(powers), keys) / summed
        mixed = dot3(split(gathered), split(wv[...]))
        result = x + dot3(split(mixed), split(wo[...]))
        attended[f] = result
        v = rms(result, gain_c[...].reshape(1, channels))
        hid[f] = (v / (1.0 + jnp.exp(-v))).reshape(rows, width, channels)
        base = 5 * f
        edge(base, hid.at[f, rows - 1], up.at[f], 0, 1)
        edge(base + 1, hid.at[f, 0], down.at[f], 0, -1)
        if f >= frames - 2:
            p = f - (frames - 2)
            edge(base + 2, hid.at[f], past.at[p], 1, 0)
            edge(base + 3, hid.at[f, rows - 1], past_up.at[p], 1, 1)
            edge(base + 4, hid.at[f, 0], past_down.at[p], 1, -1)
        for r in range(1, rows + 1):
            place(f + 2, r)
        if 1 <= f < frames - 1 and f <= CHUNKS:
            for k in later:
                arrive(f - 1, k)

    for chunk in range(CHUNKS):
        for k in early:
            arrive(chunk, k)
    for goes, comes, move, dst in edges:

        @pl.when(comes)
        def _(move=move):
            move.wait_recv()

        @pl.when(jnp.logical_not(comes))
        def _(dst=dst):
            dst[...] = jnp.zeros(dst.shape, F32)

    for f in range(frames + 2):
        for r in range(rows + 2):
            if f < 2 or r in (0, rows + 1):
                place(f, r)
    for chunk in range(CHUNKS):
        for k in later:
            arrive(chunk, k)
    own_copy.wait()
    pixels = frames * tokens
    for a in range(CHUNKS):
        for k in range(len(plan)):
            arrive(a, k)

        def row_taps(b, carry, a=a):
            block = weights[pl.ds(9 * a + 3 * b, 3)].reshape(3 * channels, channels)
            high = xh[pl.ds(a, frames), pl.ds(b, rows)].reshape(pixels, 3 * channels)
            low = xl[pl.ds(a, frames), pl.ds(b, rows)].reshape(pixels, 3 * channels)
            product = dot3((high, low), split(block))
            out[...] = out[...] + product
            return carry

        if a == 0:
            out[...] = jnp.zeros(out.shape, F32)
        lax.fori_loop(0, 3, row_taps, 0)

    for f in range(frames):
        for distance in range(1, tiles):
            for direction in (1, -1):

                @pl.when(sends(distance, direction))
                def _(f=f, distance=distance, direction=direction):
                    line(f, distance, direction).wait_send()

    for goes, comes, move, dst in edges:

        @pl.when(goes)
        def _(move=move):
            move.wait_send()

    for chunk in range(CHUNKS):
        for k in range(len(plan)):
            shard_copy(chunk, k).wait_send()


PIECES = [(9 * a + 3 * b, 3, (a, b) in ((2, 1), (1, 2), (0, 0), (0, 1))) for a in (2, 1, 0) for b in range(3)]
BLOCKS = len(PIECES)
AHEAD, LAG = 3, 2


def pair_kernel(
    act_hbm, gain_a_hbm, wq_hbm, wk_hbm, wv_hbm, wo_hbm, gain_c_hbm, kernel_hbm, attended, out,
    act, gain_a, wq, wk, wv, wo, gain_c, others, hid, ret, ret_in, weights, m1h, m1l, m2h, m2l, xh, xl,
    local_sem, line_send, line_recv, ret_send, ret_recv, gather_send, gather_recv, past_send, past_recv, shard_send, shard_recv, core_send, core_recv,
):
    frames, tokens, channels = act.shape
    width = hid.shape[2]
    rows = tokens // width
    group, me, tile = lax.axis_index("groups"), lax.axis_index("tm"), lax.axis_index("tile")
    size = kernel_hbm.shape[1]
    half, quarter = size // 2, size // 4
    inner = (tile == 1) | (tile == 2)
    outer = jnp.logical_not(inner)
    low = tile < 2
    place_in_pair = inner.astype(jnp.int32)
    core_of = me % 2
    side = (me // 2) % 2
    x_partner = {"groups": 1 - group}
    y_partner = {"tm": me + 2 - 4 * side}
    core_partner = {"tm": me + 1 - 2 * core_of}
    pair_partner = {"tile": tile + 1 - 2 * (tile % 2)}
    peer = {"tile": 3 - tile}
    later = {"tm": me + 1}
    sends_past, has_past = me < 3, me > 0

    locals_in = [(act_hbm, act), (gain_a_hbm, gain_a), (wq_hbm, wq), (wk_hbm, wk), (wv_hbm, wv), (wo_hbm, wo), (gain_c_hbm, gain_c)]
    local = [pltpu.make_async_copy(src, dst, local_sem.at[i]) for i, (src, dst) in enumerate(locals_in)]
    own_rows = weights.at[:, pl.ds(pl.multiple_of(me * size, size), size)]
    local.append(pltpu.make_async_copy(kernel_hbm, own_rows, local_sem.at[len(locals_in)]))
    for c in local:
        c.start()

    barrier = pltpu.get_barrier_semaphore()

    def greet(device):
        pl.semaphore_signal(barrier, inc=1, device_id=device, device_id_type=MESH)

    for device in (x_partner, y_partner, core_partner, pair_partner):
        greet(device)
    pl.when(inner)(lambda: greet(peer))
    crossing = me == 1, me == 2
    pl.when(crossing[0])(lambda: greet({"tm": me + 1}))
    pl.when(crossing[1])(lambda: greet({"tm": me - 1}))
    pl.semaphore_wait(barrier, 4 + inner.astype(jnp.int32) + (crossing[0] | crossing[1]).astype(jnp.int32))

    def copy(src, dst, send, recv, device):
        return pltpu.make_async_remote_copy(
            src_ref=src, dst_ref=dst, send_sem=send, recv_sem=recv, device_id=device, device_id_type=MESH
        )

    def line(f, slot):
        src = others.at[f, 0] if slot == 2 else act_hbm.at[f]
        return copy(src, others.at[f, slot], line_send.at[f, slot], line_recv.at[f, slot], pair_partner if slot == 0 else peer)

    def back(f, part):
        if part == 0:
            return copy(ret.at[f], ret_in.at[f], ret_send.at[f, 0], ret_recv.at[f, 0], pair_partner)
        near, far = jnp.where(low, 1, rows), jnp.where(low, rows + 1, 0)
        return copy(hid.at[f + 2, near], hid.at[f + 2, far], ret_send.at[f, 1], ret_recv.at[f, 1], pair_partner)

    def back_arrival(f, part):
        if part == 0:
            return copy(ret_in.at[f], ret_in.at[f], ret_send.at[f, 0], ret_recv.at[f, 0], pair_partner)
        here = hid.at[f + 2, jnp.where(low, rows + 1, 0)]
        return copy(here, here, ret_send.at[f, 1], ret_recv.at[f, 1], pair_partner)

    def gather(slot):
        src = act_hbm.at[frames - 1] if slot == 0 else others.at[frames - 1, slot]
        return copy(src, others.at[frames - 1, slot], gather_send.at[slot], gather_recv.at[slot], pair_partner)

    def past(f, kept, arriving=False):
        there = hid.at[(f - 1, kept)]
        src = there if arriving else hid.at[(f + 2, kept)]
        return copy(src, there, past_send.at[f - 1], past_recv.at[f - 1], later)

    def each_past(act_on):
        pl.when(inner)(lambda: act_on(pl.ds(0, rows + 2)))
        pl.when(outer)(lambda: act_on(pl.ds(jnp.where(low, 1, 0), rows + 1)))

    def taps_of(k):
        return pl.ds(PIECES[k][0], PIECES[k][1])

    def region(ref, k, shard, which, where):
        row = which * half
        length = half
        if where is not None:
            row, length = row + where * quarter, quarter
        if shard is not None:
            row = row + shard * size
        return ref.at[taps_of(k), pl.ds(pl.multiple_of(row, quarter), length)]

    foreign, theirs = me + 2 - 4 * side, me + 1 - 2 * core_of
    there = theirs + 2 - 4 * side

    def shard_copy(kind, k):
        q = place_in_pair if PIECES[k][2] else None
        sems = shard_send.at[kind, k], shard_recv.at[kind, k]
        if kind == 0:
            return copy(region(kernel_hbm, k, None, group, q), region(weights, k, me, group, q), *sems, y_partner)
        if kind == 1:
            ref = region(weights, k, foreign, group, q)
            return copy(ref, ref, *sems, x_partner)
        if kind in (2, 3):
            ref = region(weights, k, foreign, group if kind == 2 else 1 - group, None)
            return copy(ref, ref, *sems, core_partner)
        ref = region(weights, k, foreign, group if kind == 4 else 1 - group, q)
        return copy(ref, ref, *sems, pair_partner)

    def shard_arrival(kind, k):
        q = place_in_pair if PIECES[k][2] else None
        sems = shard_send.at[kind, k], shard_recv.at[kind, k]
        if kind == 0:
            ref, device = region(weights, k, foreign, group, q), y_partner
        elif kind == 1:
            ref, device = region(weights, k, foreign, 1 - group, q), x_partner
        elif kind in (2, 3):
            ref, device = region(weights, k, there, group if kind == 2 else 1 - group, None), core_partner
        else:
            ref, device = region(weights, k, foreign, group if kind == 4 else 1 - group, 1 - q), pair_partner
        return copy(ref, ref, *sems, device)

    started = []

    def send(kind, k):
        started.append((kind, k))
        shard_copy(kind, k).start()

    done = set()

    def step(k, stage):
        if k < 0 or (k, stage) in done:
            return
        done.add((k, stage))
        quartered = PIECES[k][2]
        if stage == 0:
            shard_arrival(0, k).wait_recv()
            if k + AHEAD < BLOCKS:
                send(0, k + AHEAD)
            send(1, k)
            send(4 if quartered else 2, k)
        elif stage == 1:
            shard_arrival(1, k).wait_recv()
            if quartered:
                send(5, k)
                shard_arrival(4, k).wait_recv()
                send(2, k)
            else:
                send(3, k)
        elif quartered:
            shard_arrival(5, k).wait_recv()
            send(3, k)

    def service(k):
        step(k, 0)
        step(k - LAG, 1)
        step(k - 2 * LAG, 2)

    core_copies = [
        copy(
            kernel_hbm.at[pl.ds(9 * a, 9)], weights.at[pl.ds(9 * a, 9), pl.ds(pl.multiple_of(me * size, size), size)],
            core_send.at[a], core_recv.at[a], core_partner,
        )
        for a in (2, 1, 0)
    ]

    def core_arrival(a):
        ref = weights.at[pl.ds(9 * a, 9), pl.ds(pl.multiple_of(theirs * size, size), size)]
        return copy(ref, ref, core_send.at[a], core_recv.at[a], core_partner)

    def ready(k):
        for earlier in range(k + 1):
            for stage in range(3):
                step(earlier, stage)
        for kind in (2, 3):
            shard_arrival(kind, k).wait_recv()
        if k == 0:
            local[-1].wait()
        if k % 3 == 0:
            core_arrival(2 - k // 3).wait_recv()

    def conv(first, count, t, times):
        def row_taps(k, carry):
            a, b = 2 - k // 3, k % 3
            block = weights[pl.ds(9 * a + 3 * b, 3)].reshape(3 * channels, channels)
            high = xh[pl.ds(t, times), pl.ds(b, rows)].reshape(times * tokens, 3 * channels)
            lo = xl[pl.ds(t, times), pl.ds(b, rows)].reshape(times * tokens, 3 * channels)
            here = pl.ds(pl.multiple_of((t - a) * tokens, tokens), times * tokens)
            out[here] = out[here] + dot3((high, lo), split(block))
            return carry

        lax.fori_loop(first, first + count, row_taps, 0)

    out[...] = jnp.zeros(out.shape, F32)

    @pl.when(inner)
    def _():
        line(0, 1).start()

    @pl.when(outer)
    def _():
        line(0, 0).start()

    for k in range(AHEAD):
        send(0, k)
    for c in core_copies:
        c.start()

    for c in local[:-1]:
        c.wait()
    gain = gain_a[...].reshape(1, channels)
    gain_2 = gain_c[...].reshape(1, channels)

    @pl.when(outer)
    def _():
        line(0, 0).wait_send()
        line(1, 0).start()

    m1 = dot3(split(wq[...]), split(wk[...]), TRANSPOSED) * (1.0 / math.sqrt(channels))
    m1h[...], m1l[...] = split(m1)
    m2h[...], m2l[...] = split(dot3(split(wv[...]), split(wo[...])))

    @pl.when(inner)
    def _():
        line(0, 0).wait_recv()
        line(0, 2).start()

    cell = lax.broadcasted_iota(jnp.int32, (width, channels), 0)

    def place(t, r):
        value = hid[t, r]
        before = jnp.where(cell == 0, 0.0, pltpu.roll(value, 1, 0))
        after = jnp.where(cell == width - 1, 0.0, pltpu.roll(value, width - 1, 0))
        for c, v in enumerate((before, value, after)):
            xh[t, r, :, c * channels : (c + 1) * channels], xl[t, r, :, c * channels : (c + 1) * channels] = split(v)

    def activate(v):
        v = rms(v, gain_2)
        return v / (1.0 + jnp.exp(-v))

    def attend(f, asked, seen):
        cells = [split(rms(v, gain)) for v in seen]
        keys = tuple(jnp.concatenate([c[i] for c in cells], axis=0) for i in range(2))
        folded = split(dot3(split(rms(asked, gain)), (m1h[...], m1l[...])))
        scores = dot3(folded, keys, TRANSPOSED)
        powers = jnp.exp(scores - jnp.max(scores, axis=-1, keepdims=True))
        summed = jnp.sum(powers, axis=-1, keepdims=True)
        gathered = dot3(split(powers), keys) / summed
        return asked + dot3(split(gathered), (m2h[...], m2l[...]))

    def row_of(f, slot, first):
        return others[f, slot, pl.ds(pl.multiple_of(jnp.where(first, 0, tokens - width), width), width)]

    def attend_inner(f):
        own, last = act[f], f == frames - 1
        partner = row_of(f, 0, jnp.logical_not(low)) if last else others[f, 0]
        asked = jnp.concatenate([own, partner, row_of(f, 1, low)], axis=0)
        result = attend(f, asked, (own, others[f, 0], others[f, 1], others[f, 2]))
        if not last:
            ret[f] = result[tokens : 2 * tokens]
            back(f, 0).start()
        hidden = activate(result)
        hid[f + 2, 1 : rows + 1] = hidden[:tokens].reshape(rows, width, channels)
        if not last:
            back(f, 1).start()
        attended[f] = result[:tokens]
        edge = hidden[tokens : tokens + width]
        if not last:
            edge = jnp.where(low, hidden[2 * tokens - width : 2 * tokens], edge)
        beyond = hidden[-width:]
        hid[f + 2, 0] = jnp.where(low, edge, beyond)
        hid[f + 2, rows + 1] = jnp.where(low, beyond, edge)

    def attend_outer(f):
        for slot in range(3):
            gather(slot).wait_recv()
        own = act[f]
        asked = jnp.concatenate([own, row_of(f, 0, low)], axis=0)
        result = attend(f, asked, (own, others[f, 0], others[f, 1], others[f, 2]))
        hidden = activate(result)
        hid[f + 2, 1 : rows + 1] = hidden[:tokens].reshape(rows, width, channels)
        hid[f + 2, jnp.where(low, rows + 1, 0)] = hidden[tokens:]
        hid[f + 2, jnp.where(low, 0, rows + 1)] = jnp.zeros((width, channels), F32)
        attended[f] = result[:tokens]

    def receive(f):
        back_arrival(f, 0).wait_recv()
        result = ret_in[f]
        attended[f] = result
        hid[f + 2, 1 : rows + 1] = activate(result).reshape(rows, width, channels)
        hid[f + 2, jnp.where(low, 0, rows + 1)] = jnp.zeros((width, channels), F32)
        back_arrival(f, 1).wait_recv()

    def settle(f, kept):
        if f > 0:

            @pl.when(sends_past)
            def _():
                past(f, kept).start()

        for r in range(rows + 2):
            place(f + 2, r)

    every, kept_outer = pl.ds(0, rows + 2), pl.ds(jnp.where(low, 1, 0), rows + 1)

    for f in range(frames):

        @pl.when(inner)
        def _():
            line(f, 1).wait_recv()
            if f + 1 < frames:
                line(f + 1, 1).start()
            else:
                gather(1).start()

        if f == 0:

            @pl.when(outer)
            def _():
                line(1, 0).wait_send()
                line(2, 0).start()

        service(2 * f)
        if f == frames - 1:
            ready(0)
            ready(1)

            @pl.when(inner)
            def _():
                conv(0, 2, 2, 2)

        @pl.when(inner)
        def _():
            line(f, 2).wait_recv()
            if f + 1 < frames:
                line(f + 1, 0).wait_recv()
                line(f + 1, 2).start()
            else:
                gather(2).start()
            attend_inner(f)
            settle(f, every)
            if f == frames - 2:
                gather(0).start()

        if f > 0:

            @pl.when(outer)
            def _():
                receive(f - 1)
                settle(f - 1, kept_outer)
                if f == frames - 1:
                    conv(0, 2, 2, 2)

        service(2 * f + 1)

    @pl.when(outer)
    def _():
        attend_outer(frames - 1)
        settle(frames - 1, kept_outer)

    service(6)
    ready(2)
    conv(2, 1, 2, 2)
    conv(0, 3, 4, 1)
    for k in (7, 8):
        service(k)
    for k in (3, 4, 5):
        ready(k)
    conv(3, 3, 2, 2)

    def arrive(kept):
        past(1, kept, True).wait_recv()
        past(2, kept, True).wait_recv()

    @pl.when(has_past)
    def _():
        each_past(arrive)

        @pl.when(outer)
        def _():
            for t in range(2):
                hid[t, jnp.where(low, 0, rows + 1)] = jnp.zeros((width, channels), F32)

    @pl.when(jnp.logical_not(has_past))
    def _():
        hid[0:2] = jnp.zeros((2, *hid.shape[1:]), F32)

    for t in range(2):
        for r in range(rows + 2):
            place(t, r)
    conv(3, 3, 1, 1)
    ready(6)
    conv(6, 1, 0, 3)
    ready(7)
    conv(7, 1, 0, 3)
    ready(8)
    conv(8, 1, 0, 3)

    @pl.when(inner)
    def _():
        for f in range(frames):
            line(f, 1).wait_send()
            line(f, 2).wait_send()
            if f + 1 < frames:
                back(f, 0).wait_send()
                back(f, 1).wait_send()
        for slot in range(3):
            gather(slot).wait_send()

    @pl.when(outer)
    def _():
        line(2, 0).wait_send()

    def leave(kept):
        past(1, kept).wait_send()
        past(2, kept).wait_send()

    pl.when(sends_past)(lambda: each_past(leave))
    for c in core_copies:
        c.wait_send()
    for kind, k in started:
        shard_copy(kind, k).wait_send()


def paired(own, gain_attention, w_query, w_key, w_value, w_out, gain_conv, conv_weight, rows):
    frames, tokens, channels = own.shape
    width = tokens // rows
    taps = conv_weight.shape[0]
    vmem, dma = pltpu.VMEM, pltpu.SemaphoreType.DMA
    return pl.pallas_call(
        pair_kernel,
        in_specs=[pl.BlockSpec(memory_space=pl.ANY)] * 8,
        out_specs=[pl.BlockSpec(memory_space=pltpu.VMEM)] * 2,
        out_shape=[
            jax.ShapeDtypeStruct(own.shape, F32),
            jax.ShapeDtypeStruct((frames * tokens, channels), F32),
        ],
        scratch_shapes=[
            vmem(own.shape, F32),
            vmem((channels,), F32),
            *[vmem((channels, channels), F32)] * 4,
            vmem((channels,), F32),
            vmem((frames, 3, tokens, channels), F32),
            vmem((frames + 2, rows + 2, width, channels), F32),
            vmem((frames, tokens, channels), F32),
            vmem((frames, tokens, channels), F32),
            vmem((taps, channels, channels), F32),
            *[vmem((channels, channels), BF16)] * 4,
            *[vmem((frames + 2, rows + 2, width, 3 * channels), BF16)] * 2,
            dma((8,)),
            dma((frames, 3)),
            dma((frames, 3)),
            dma((frames, 2)),
            dma((frames, 2)),
            dma((3,)),
            dma((3,)),
            dma((2,)),
            dma((2,)),
            dma((6, BLOCKS)),
            dma((6, BLOCKS)),
            dma((3,)),
            dma((3,)),
        ],
        compiler_params=pltpu.CompilerParams(
            collective_id=0, has_side_effects=True, vmem_limit_bytes=VMEM_LIMIT
        ),
    )(own, gain_attention, w_query, w_key, w_value, w_out, gain_conv, conv_weight)


def body(activations, gain_attention, w_query, w_key, w_value, w_out, gain_conv, conv_weight):
    frames, rows, width, channels = activations.shape
    tokens = rows * width
    own = activations.reshape(frames, tokens, channels)
    times, tiles = lax.axis_size("tm"), lax.axis_size("tile")
    taps, size = conv_weight.shape[:2]
    if (lax.axis_size("groups"), times, tiles) == (2, 4, 4) and (frames, rows, taps) == (3, 2, 27) and size % 32 == 0:
        attended, conv_out = paired(
            own, gain_attention, w_query, w_key, w_value, w_out, gain_conv, conv_weight, rows
        )
        return (attended.reshape(activations.shape), conv_out.reshape(activations.shape))
    plan = shard_plan(times, lax.axis_size("groups") == 2 and size % 16 == 0)
    vmem = pl.BlockSpec(memory_space=pltpu.VMEM)
    dma = pltpu.SemaphoreType.DMA
    attended, conv_out = pl.pallas_call(
        functools.partial(kernel, plan, times, tiles),
        in_specs=[vmem] * 7 + [pl.BlockSpec(memory_space=pl.ANY)],
        out_specs=[vmem, vmem],
        out_shape=[
            jax.ShapeDtypeStruct(own.shape, F32),
            jax.ShapeDtypeStruct((frames * tokens, channels), F32),
        ],
        scratch_shapes=[
            pltpu.VMEM((frames, tiles - 1, tokens, channels), F32),
            pltpu.VMEM((frames, rows, width, channels), F32),
            pltpu.VMEM((frames, width, channels), F32),
            pltpu.VMEM((frames, width, channels), F32),
            pltpu.VMEM((2, rows, width, channels), F32),
            pltpu.VMEM((2, width, channels), F32),
            pltpu.VMEM((2, width, channels), F32),
            pltpu.VMEM((taps, channels, channels), F32),
            pltpu.VMEM((frames + 2, rows + 2, width, 3 * channels), BF16),
            pltpu.VMEM((frames + 2, rows + 2, width, 3 * channels), BF16),
            dma((frames, 2, tiles - 1)),
            dma((frames, tiles - 1)),
            dma((5 * frames,)),
            dma((5 * frames,)),
            dma((CHUNKS, len(plan))),
            dma((CHUNKS, len(plan))),
            dma,
        ],
        compiler_params=pltpu.CompilerParams(
            collective_id=0, has_side_effects=True, vmem_limit_bytes=VMEM_LIMIT
        ),
    )(
        own, gain_attention, w_query, w_key, w_value, w_out, gain_conv, conv_weight
    )
    return (attended.reshape(activations.shape), conv_out.reshape(activations.shape))


def solution(mesh):
    placed = P(("groups", "tm"), "tile", None, None)
    return jax.shard_map(
        body,
        mesh=mesh,
        in_specs=(placed, P(), P(), P(), P(), P(), P(), P(None, "tm", None)),
        out_specs=(placed, placed),
        check_vma=False,
    )
```

```python
import functools
import math

import jax
import jax.numpy as jnp
from jax import lax
from jax.experimental import pallas as pl
from jax.experimental.pallas import tpu as pltpu
from jax.sharding import PartitionSpec as P

F32, BF16 = jnp.float32, jnp.bfloat16
VMEM_LIMIT = 56 * 1024 * 1024
CHUNKS = 3


def split(x):
    high = x.astype(BF16)
    return high, (x - high.astype(F32)).astype(BF16)


def dot3(a, b, dims=(((1,), (0,)), ((), ()))):
    dot = functools.partial(lax.dot_general, dimension_numbers=dims, preferred_element_type=F32)
    (ah, al), (bh, bl) = a, b
    return dot(ah, bh) + (dot(ah, bl) + dot(al, bh))


TRANSPOSED = (((1,), (1,)), ((), ()))


def rms(v, gain):
    return v * lax.rsqrt(jnp.mean(v * v, axis=-1, keepdims=True) + 1e-06) * gain


MESH = pl.DeviceIdType.MESH


def shard_plan(shards, halved):
    plan, held = [], [(0, 0, None)]
    bit = 1
    while 2 * bit < shards:
        bit *= 2
    while bit >= 1 and shards > 1:
        arrived = []
        for mask, part, source in held:
            if halved and bit > 1 and part == 0:
                plan.append(("tm", bit, mask, 1, source))
                plan.append(("groups", 1, mask ^ bit, 1, len(plan) - 1))
                arrived += [(mask ^ bit, 1, len(plan) - 2), (mask ^ bit, 2, len(plan) - 1)]
            else:
                plan.append(("tm", bit, mask, part, source))
                arrived.append((mask ^ bit, part, len(plan) - 1))
        held += arrived
        bit //= 2
    return plan


def kernel(
    plan, times, tiles, act, gain_a, wq, wk, wv, wo, gain_c, kernel_hbm, attended, out,
    others, hid, up, down, past, past_up, past_down, weights, xh, xl,
    line_send, line_recv, edge_send, edge_recv, shard_send, shard_recv, own_sem,
):
    frames, rows, width, channels = hid.shape
    tokens = rows * width
    group, me, tile = lax.axis_index("groups"), lax.axis_index("tm"), lax.axis_index("tile")
    size = kernel_hbm.shape[1]
    half = size // 2

    barrier = pltpu.get_barrier_semaphore()
    friends = [(True, {"groups": 1 - group})]
    bit = 1
    while bit < times:
        friends.append((True, {"tm": me + bit * (1 - 2 * ((me // bit) % 2))}))
        bit *= 2
    for dt, dz in ((0, 1), (1, 0), (1, 1), (1, -1)):
        for sign in (1, -1):
            t, z = me + sign * dt, tile + sign * dz
            inside = (t >= 0) & (t < times) & (z >= 0) & (z < tiles)
            friends.append((inside, {"tm": t, "tile": z}))
    count = 0
    for inside, device in friends:
        if inside is True:
            pl.semaphore_signal(barrier, inc=1, device_id=device, device_id_type=MESH)
            count = count + 1
        else:

            @pl.when(inside)
            def _(device=device):
                pl.semaphore_signal(barrier, inc=1, device_id=device, device_id_type=MESH)

            count = count + inside.astype(jnp.int32)
    pl.semaphore_wait(barrier, count)

    def copy(src, dst, send, recv, device):
        return pltpu.make_async_remote_copy(
            src_ref=src, dst_ref=dst, send_sem=send, recv_sem=recv, device_id=device, device_id_type=MESH
        )

    def line(f, distance, direction):
        slot_here = distance - 1 if direction > 0 else tiles - distance + 1
        slot_there = distance if direction > 0 else tiles - distance
        src = act.at[f] if distance == 1 else others.at[f, slot_here - 1]
        side = 0 if direction > 0 else 1
        return copy(
            src, others.at[f, slot_there - 1], line_send.at[f, side, distance - 1],
            line_recv.at[f, slot_there - 1], {"tile": tile + direction},
        )

    def sends(distance, direction):
        if direction > 0:
            return (tile >= distance - 1) & (tile < tiles - 1)
        return (tile + distance - 1 <= tiles - 1) & (tile > 0)

    def flip(value, bit):
        return value + bit * (1 - 2 * ((value // bit) % 2))

    def flipped(mask):
        value, bit = me, 1
        while bit <= mask:
            if mask & bit:
                value = flip(value, bit)
            bit *= 2
        return value

    def region(ref, chunk, shard, part, swap, local=False):
        first = group if not swap else 1 - group
        start = {0: 0, 1: first * half, 2: (1 - first) * half}[part]
        row = start if local else shard * size + start
        length = size if part == 0 else half
        if not isinstance(row, int):
            row = pl.multiple_of(row, math.gcd(size, length))
        return ref.at[pl.ds(9 * chunk, 9), pl.ds(row, length)]

    def shard_copy(chunk, k):
        axis, bit, mask, part, source = plan[k]
        there = region(weights, chunk, flipped(mask), part, False)
        src = region(kernel_hbm, chunk, 0, part, False, True) if mask == 0 else there
        device = {"tm": flip(me, bit)} if axis == "tm" else {"groups": 1 - group}
        return copy(src, there, shard_send.at[chunk, k], shard_recv.at[chunk, k], device)

    def shard_arrival(chunk, k):
        axis, bit, mask, part, source = plan[k]
        if axis == "tm":
            here, device = region(weights, chunk, flipped(mask ^ bit), part, False), {"tm": flip(me, bit)}
        else:
            here, device = region(weights, chunk, flipped(mask), part, True), {"groups": 1 - group}
        return copy(here, here, shard_send.at[chunk, k], shard_recv.at[chunk, k], device)

    early = [k for k, step in enumerate(plan) if step[4] is None and any(s[4] == k for s in plan)]
    later = [k for k, step in enumerate(plan) if step[4] is not None and any(s[4] == k for s in plan)]

    waited = set()

    def arrive(chunk, k):
        if (chunk, k) in waited:
            return
        waited.add((chunk, k))
        shard_arrival(chunk, k).wait_recv()
        if k in early and chunk + 1 < CHUNKS:
            shard_copy(chunk + 1, k).start()
        for j, step in enumerate(plan):
            if step[4] == k:
                shard_copy(chunk, j).start()

    def start_line(f):
        for direction in (1, -1):

            @pl.when(sends(1, direction))
            def _(direction=direction):
                line(f, 1, direction).start()

    start_line(0)
    for chunk in range(CHUNKS):
        for k, step in enumerate(plan):
            if step[4] is None and (chunk == 0 or k not in early):
                shard_copy(chunk, k).start()
    own_rows = weights.at[:, pl.ds(pl.multiple_of(me * size, size), size)]
    own_copy = pltpu.make_async_copy(kernel_hbm, own_rows, own_sem)
    own_copy.start()

    cell = lax.broadcasted_iota(jnp.int32, (width, channels), 0)

    def place(f, r):
        upper, middle, lower, t = (past_up, past, past_down, f) if f < 2 else (up, hid, down, f - 2)
        value = upper[t] if r == 0 else lower[t] if r == rows + 1 else middle[t, r - 1]
        before = jnp.where(cell == 0, 0.0, pltpu.roll(value, 1, 0))
        after = jnp.where(cell == width - 1, 0.0, pltpu.roll(value, width - 1, 0))
        for c, v in enumerate((before, value, after)):
            high, low = split(v)
            xh[f, r, :, c * channels : (c + 1) * channels] = high
            xl[f, r, :, c * channels : (c + 1) * channels] = low

    gain = gain_a[...].reshape(1, channels)
    scale = 1.0 / math.sqrt(channels)
    edges = []

    def edge(number, src, dst, dt, dz):
        t, z = me + dt, tile + dz
        goes = (t < times) & (z >= 0) & (z < tiles)
        comes = (me - dt >= 0) & (tile - dz >= 0) & (tile - dz < tiles)
        move = copy(src, dst, edge_send.at[number], edge_recv.at[number], {"tm": t, "tile": z})

        @pl.when(goes)
        def _():
            move.start()

        edges.append((goes, comes, move, dst))

    for f in range(frames):
        for distance in range(1, tiles):
            for direction in (1, -1):
                comes = tile >= distance if direction > 0 else tile + distance < tiles

                @pl.when(comes)
                def _(f=f, distance=distance, direction=direction):
                    slot = distance if direction > 0 else tiles - distance
                    here = others.at[f, slot - 1]
                    side = 0 if direction > 0 else 1
                    copy(
                        here, here, line_send.at[f, side, distance - 1], line_recv.at[f, slot - 1],
                        {"tile": tile - direction},
                    ).wait_recv()

                if distance + 1 < tiles:

                    @pl.when(sends(distance + 1, direction))
                    def _(f=f, distance=distance, direction=direction):
                        line(f, distance + 1, direction).start()

            if distance == 1 and f + 1 < frames:
                start_line(f + 1)
        if tiles == 1 and f + 1 < frames:
            start_line(f + 1)
        if f < CHUNKS and f < frames - 1:
            for k in early:
                arrive(f, k)
        x = act[f]
        normed = split(rms(x, gain))
        queries = dot3(normed, split(wq[...]))
        folded = split(dot3(split(queries), split(wk[...]), TRANSPOSED))
        cells = [normed] + [split(rms(others[f, s], gain)) for s in range(tiles - 1)]
        keys = tuple(jnp.concatenate([c[i] for c in cells], axis=0) for i in range(2))
        scores = dot3(folded, keys, TRANSPOSED) * scale
        powers = jnp.exp(scores - jnp.max(scores, axis=-1, keepdims=True))
        summed = jnp.sum(powers, axis=-1, keepdims=True)
        gathered = dot3(split(powers), keys) / summed
        mixed = dot3(split(gathered), split(wv[...]))
        result = x + dot3(split(mixed), split(wo[...]))
        attended[f] = result
        v = rms(result, gain_c[...].reshape(1, channels))
        hid[f] = (v / (1.0 + jnp.exp(-v))).reshape(rows, width, channels)
        base = 5 * f
        edge(base, hid.at[f, rows - 1], up.at[f], 0, 1)
        edge(base + 1, hid.at[f, 0], down.at[f], 0, -1)
        if f >= frames - 2:
            p = f - (frames - 2)
            edge(base + 2, hid.at[f], past.at[p], 1, 0)
            edge(base + 3, hid.at[f, rows - 1], past_up.at[p], 1, 1)
            edge(base + 4, hid.at[f, 0], past_down.at[p], 1, -1)
        for r in range(1, rows + 1):
            place(f + 2, r)
        if 1 <= f < frames - 1 and f <= CHUNKS:
            for k in later:
                arrive(f - 1, k)

    for chunk in range(CHUNKS):
        for k in early:
            arrive(chunk, k)
    for goes, comes, move, dst in edges:

        @pl.when(comes)
        def _(move=move):
            move.wait_recv()

        @pl.when(jnp.logical_not(comes))
        def _(dst=dst):
            dst[...] = jnp.zeros(dst.shape, F32)

    for f in range(frames + 2):
        for r in range(rows + 2):
            if f < 2 or r in (0, rows + 1):
                place(f, r)
    for chunk in range(CHUNKS):
        for k in later:
            arrive(chunk, k)
    own_copy.wait()
    pixels = frames * tokens
    for a in range(CHUNKS):
        for k in range(len(plan)):
            arrive(a, k)

        def row_taps(b, carry, a=a):
            block = weights[pl.ds(9 * a + 3 * b, 3)].reshape(3 * channels, channels)
            high = xh[pl.ds(a, frames), pl.ds(b, rows)].reshape(pixels, 3 * channels)
            low = xl[pl.ds(a, frames), pl.ds(b, rows)].reshape(pixels, 3 * channels)
            product = dot3((high, low), split(block))
            out[...] = out[...] + product
            return carry

        if a == 0:
            out[...] = jnp.zeros(out.shape, F32)
        lax.fori_loop(0, 3, row_taps, 0)

    for f in range(frames):
        for distance in range(1, tiles):
            for direction in (1, -1):

                @pl.when(sends(distance, direction))
                def _(f=f, distance=distance, direction=direction):
                    line(f, distance, direction).wait_send()

    for goes, comes, move, dst in edges:

        @pl.when(goes)
        def _(move=move):
            move.wait_send()

    for chunk in range(CHUNKS):
        for k in range(len(plan)):
            shard_copy(chunk, k).wait_send()


BLOCKS, AHEAD = 9, 3
QUARTERED = (0, 1, 7, 8)
INNER_ORDER = (
    ("gat", 0), ("pre",), ("fwd", 0), ("W", 0, 0), ("own", 1), ("W", 1, 0), ("fwd", 1), ("W", 2, 0), ("W", 0, 1),
    ("W", 1, 1), ("att", 0), ("own", 2), ("W", 3, 0), ("att", 1), ("W", 2, 1), ("W", 0, 2), ("fwd", 2), ("W", 1, 2),
    ("W", 4, 0), ("W", 5, 0), ("W", 0, 3), ("gat", 1), ("W", 3, 1), ("gat", 2), ("W", 6, 0), ("W", 4, 1),
    ("att", 2), ("W", 1, 3), ("conv", 0, 1, 2, 3), ("conv", 1, 1, 2, 2), ("W", 7, 0), ("past", 1), ("W", 5, 1),
    ("W", 6, 1), ("W", 8, 0), ("conv", 3, 1, 2, 2), ("conv", 2, 1, 2, 3), ("W", 7, 1), ("conv", 1, 1, 4, 1),
    ("W", 7, 2), ("conv", 4, 1, 2, 2), ("W", 8, 1), ("past", 2), ("conv", 4, 1, 1, 1), ("W", 7, 3),
    ("conv", 5, 1, 1, 3), ("W", 8, 2), ("W", 8, 3), ("conv", 3, 1, 1, 1), ("conv", 6, 2, 0, 3),
    ("conv", 8, 1, 2, 1), ("conv", 8, 1, 0, 2),
)
OUTER_ORDER = (
    ("W", 0, 0), ("W", 1, 0), ("W", 0, 1), ("W", 2, 0), ("W", 3, 0), ("W", 0, 2), ("W", 1, 1), ("W", 2, 1),
    ("W", 4, 0), ("W", 1, 2), ("W", 5, 0), ("W", 0, 3), ("pre",), ("W", 6, 0), ("att", 0), ("W", 1, 3), ("W", 3, 1),
    ("W", 4, 1), ("att", 1), ("conv", 3, 1, 2, 2), ("conv", 2, 1, 2, 2), ("W", 7, 0), ("W", 5, 1), ("W", 6, 1),
    ("conv", 4, 1, 2, 2), ("W", 8, 0), ("conv", 5, 1, 2, 2), ("past", 1), ("W", 7, 1), ("att", 2), ("W", 7, 2),
    ("W", 8, 1), ("conv", 2, 1, 4, 1), ("conv", 6, 1, 2, 1), ("conv", 1, 1, 2, 3), ("conv", 0, 1, 2, 3),
    ("W", 8, 2), ("past", 2), ("conv", 5, 1, 1, 1), ("W", 7, 3), ("conv", 4, 1, 1, 1), ("conv", 6, 1, 0, 2),
    ("conv", 3, 1, 1, 1), ("W", 8, 3), ("conv", 7, 2, 0, 3),
)


def first_tap(k):
    return 9 * (2 - k // 3) + 3 * (k % 3)


def pair_kernel(
    act_hbm, gain_a_hbm, wq_hbm, wk_hbm, wv_hbm, wo_hbm, gain_c_hbm, kernel_hbm, attended, out,
    act, gain_a, wq, wk, wv, wo, gain_c, others, hid, ret, ret_in, weights, m1h, m1l, m2h, m2l, xh, xl,
    local_sem, line_send, line_recv, ret_send, ret_recv, gather_send, gather_recv, past_send, past_recv, shard_send, shard_recv, core_send, core_recv,
):
    frames, tokens, channels = act.shape
    width = hid.shape[2]
    rows = tokens // width
    group, me, tile = lax.axis_index("groups"), lax.axis_index("tm"), lax.axis_index("tile")
    size = kernel_hbm.shape[1]
    half, quarter = size // 2, size // 4
    inner = (tile == 1) | (tile == 2)
    outer = jnp.logical_not(inner)
    low = tile < 2
    place_in_pair = inner.astype(jnp.int32)
    core_of = me % 2
    side = (me // 2) % 2
    x_partner = {"groups": 1 - group}
    y_partner = {"tm": me + 2 - 4 * side}
    core_partner = {"tm": me + 1 - 2 * core_of}
    pair_partner = {"tile": tile + 1 - 2 * (tile % 2)}
    peer = {"tile": 3 - tile}
    later = {"tm": me + 1}
    sends_past, has_past = me < 3, me > 0

    locals_in = [(act_hbm, act), (gain_a_hbm, gain_a), (wq_hbm, wq), (wk_hbm, wk), (wv_hbm, wv), (wo_hbm, wo), (gain_c_hbm, gain_c)]
    local = [pltpu.make_async_copy(src, dst, local_sem.at[i]) for i, (src, dst) in enumerate(locals_in)]
    own_rows = weights.at[:, pl.ds(pl.multiple_of(me * size, size), size)]
    local.append(pltpu.make_async_copy(kernel_hbm, own_rows, local_sem.at[len(locals_in)]))
    for c in local:
        c.start()

    barrier = pltpu.get_barrier_semaphore()

    def greet(device):
        pl.semaphore_signal(barrier, inc=1, device_id=device, device_id_type=MESH)

    for device in (x_partner, y_partner, core_partner, pair_partner):
        greet(device)
    pl.when(inner)(lambda: greet(peer))
    crossing = me == 1, me == 2
    pl.when(crossing[0])(lambda: greet({"tm": me + 1}))
    pl.when(crossing[1])(lambda: greet({"tm": me - 1}))
    pl.semaphore_wait(barrier, 4 + inner.astype(jnp.int32) + (crossing[0] | crossing[1]).astype(jnp.int32))

    def copy(src, dst, send, recv, device):
        return pltpu.make_async_remote_copy(
            src_ref=src, dst_ref=dst, send_sem=send, recv_sem=recv, device_id=device, device_id_type=MESH
        )

    def line(f, slot):
        src = others.at[f, 0] if slot == 2 else act_hbm.at[f]
        return copy(src, others.at[f, slot], line_send.at[f, slot], line_recv.at[f, slot], pair_partner if slot == 0 else peer)

    def back(f, part):
        if part == 0:
            return copy(ret.at[f], ret_in.at[f], ret_send.at[f, 0], ret_recv.at[f, 0], pair_partner)
        near, far = jnp.where(low, 1, rows), jnp.where(low, rows + 1, 0)
        return copy(hid.at[f + 2, near], hid.at[f + 2, far], ret_send.at[f, 1], ret_recv.at[f, 1], pair_partner)

    def back_arrival(f, part):
        if part == 0:
            return copy(ret_in.at[f], ret_in.at[f], ret_send.at[f, 0], ret_recv.at[f, 0], pair_partner)
        here = hid.at[f + 2, jnp.where(low, rows + 1, 0)]
        return copy(here, here, ret_send.at[f, 1], ret_recv.at[f, 1], pair_partner)

    def gather(slot):
        src = act_hbm.at[frames - 1] if slot == 0 else others.at[frames - 1, slot]
        return copy(src, others.at[frames - 1, slot], gather_send.at[slot], gather_recv.at[slot], pair_partner)

    def past(f, kept, arriving=False):
        there = hid.at[(f - 1, kept)]
        src = there if arriving else hid.at[(f + 2, kept)]
        return copy(src, there, past_send.at[f - 1], past_recv.at[f - 1], later)

    def each_past(act_on):
        pl.when(inner)(lambda: act_on(pl.ds(0, rows + 2)))
        pl.when(outer)(lambda: act_on(pl.ds(jnp.where(low, 1, 0), rows + 1)))

    def taps_of(k):
        return pl.ds(first_tap(k), 3)

    def region(ref, k, shard, which, where):
        row = which * half
        length = half
        if where is not None:
            row, length = row + where * quarter, quarter
        if shard is not None:
            row = row + shard * size
        return ref.at[taps_of(k), pl.ds(pl.multiple_of(row, quarter), length)]

    foreign, theirs = me + 2 - 4 * side, me + 1 - 2 * core_of
    there = theirs + 2 - 4 * side

    def shard_copy(kind, k):
        q = place_in_pair if k in QUARTERED else None
        sems = shard_send.at[kind, k], shard_recv.at[kind, k]
        if kind == 0:
            return copy(region(kernel_hbm, k, None, group, q), region(weights, k, me, group, q), *sems, y_partner)
        if kind == 1:
            ref = region(weights, k, foreign, group, q)
            return copy(ref, ref, *sems, x_partner)
        if kind in (2, 3):
            ref = region(weights, k, foreign, group if kind == 2 else 1 - group, None)
            return copy(ref, ref, *sems, core_partner)
        ref = region(weights, k, foreign, group if kind == 4 else 1 - group, q)
        return copy(ref, ref, *sems, pair_partner)

    def shard_arrival(kind, k):
        q = place_in_pair if k in QUARTERED else None
        sems = shard_send.at[kind, k], shard_recv.at[kind, k]
        if kind == 0:
            ref, device = region(weights, k, foreign, group, q), y_partner
        elif kind == 1:
            ref, device = region(weights, k, foreign, 1 - group, q), x_partner
        elif kind in (2, 3):
            ref, device = region(weights, k, there, group if kind == 2 else 1 - group, None), core_partner
        else:
            ref, device = region(weights, k, foreign, group if kind == 4 else 1 - group, 1 - q), pair_partner
        return copy(ref, ref, *sems, device)

    def send(kind, k):
        shard_copy(kind, k).start()

    def step(k, stage):
        quartered = k in QUARTERED
        if stage == 0:
            shard_arrival(0, k).wait_recv()
            if k + AHEAD < BLOCKS:
                send(0, k + AHEAD)
            send(1, k)
            send(4 if quartered else 2, k)
        elif stage == 1:
            shard_arrival(1, k).wait_recv()
            send(5 if quartered else 3, k)
        elif quartered:
            shard_arrival(4 if stage == 2 else 5, k).wait_recv()
            send(stage, k)

    core_copies = [
        copy(
            kernel_hbm.at[pl.ds(9 * a, 9)], weights.at[pl.ds(9 * a, 9), pl.ds(pl.multiple_of(me * size, size), size)],
            core_send.at[a], core_recv.at[a], core_partner,
        )
        for a in (2, 1, 0)
    ]

    def core_arrival(a):
        ref = weights.at[pl.ds(9 * a, 9), pl.ds(pl.multiple_of(theirs * size, size), size)]
        return copy(ref, ref, core_send.at[a], core_recv.at[a], core_partner)

    def conv(first, count, t, times):
        a = 2 - first // 3

        def row_taps(k, carry):
            b = k % 3
            high, low_part = split(weights[pl.ds(9 * a + 3 * b, 3)].reshape(3 * channels, channels))
            x_high = xh[t : t + times, pl.ds(b, rows)].reshape(times * tokens, 3 * channels)
            x_low = xl[t : t + times, pl.ds(b, rows)].reshape(times * tokens, 3 * channels)
            both = jnp.dot(x_high, jnp.concatenate([high, low_part], axis=1), preferred_element_type=F32)
            rest = jnp.dot(x_low, high, preferred_element_type=F32)
            here = slice((t - a) * tokens, (t - a + times) * tokens)
            out[here] = out[here] + (both[:, :channels] + (both[:, channels:] + rest))
            return carry

        if count == 1:
            row_taps(first, 0)
        else:
            lax.fori_loop(first, first + count, row_taps, 0)

    @pl.when(inner)
    def _():
        line(0, 1).start()

    @pl.when(outer)
    def _():
        for f in range(frames):
            line(f, 0).start()

    for k in range(AHEAD):
        send(0, k)
    for c in core_copies:
        c.start()
    out[...] = jnp.zeros(out.shape, F32)

    cell = lax.broadcasted_iota(jnp.int32, (width, channels), 0)

    def place(t, r):
        value = hid[t, r]
        before = jnp.where(cell == 0, 0.0, pltpu.roll(value, 1, 0))
        after = jnp.where(cell == width - 1, 0.0, pltpu.roll(value, width - 1, 0))
        for c, v in enumerate((before, value, after)):
            xh[t, r, :, c * channels : (c + 1) * channels], xl[t, r, :, c * channels : (c + 1) * channels] = split(v)

    def activate(v):
        v = rms(v, gain_c[...].reshape(1, channels))
        return v / (1.0 + jnp.exp(-v))

    def attend(f, asked, seen):
        gain = gain_a[...].reshape(1, channels)
        cells = [split(rms(v, gain)) for v in seen]
        keys = tuple(jnp.concatenate([c[i] for c in cells], axis=0) for i in range(2))
        folded = split(dot3(split(rms(asked, gain)), (m1h[...], m1l[...])))
        scores = dot3(folded, keys, TRANSPOSED)
        powers = jnp.exp(scores - jnp.max(scores, axis=-1, keepdims=True))
        summed = jnp.sum(powers, axis=-1, keepdims=True)
        gathered = dot3(split(powers), keys) / summed
        return asked + dot3(split(gathered), (m2h[...], m2l[...]))

    def row_of(f, slot, first):
        return others[f, slot, pl.ds(pl.multiple_of(jnp.where(first, 0, tokens - width), width), width)]

    def attend_inner(f):
        own, last = act[f], f == frames - 1
        partner = row_of(f, 0, jnp.logical_not(low)) if last else others[f, 0]
        asked = jnp.concatenate([own, partner, row_of(f, 1, low)], axis=0)
        result = attend(f, asked, (own, others[f, 0], others[f, 1], others[f, 2]))
        if not last:
            ret[f] = result[tokens : 2 * tokens]
            back(f, 0).start()
        hidden = activate(result)
        hid[f + 2, 1 : rows + 1] = hidden[:tokens].reshape(rows, width, channels)
        if not last:
            back(f, 1).start()
        attended[f] = result[:tokens]
        edge = hidden[tokens : tokens + width]
        if not last:
            edge = jnp.where(low, hidden[2 * tokens - width : 2 * tokens], edge)
        beyond = hidden[-width:]
        hid[f + 2, 0] = jnp.where(low, edge, beyond)
        hid[f + 2, rows + 1] = jnp.where(low, beyond, edge)

    def attend_outer(f):
        own = act[f]
        asked = jnp.concatenate([own, row_of(f, 0, low)], axis=0)
        result = attend(f, asked, (own, others[f, 0], others[f, 1], others[f, 2]))
        hidden = activate(result)
        hid[f + 2, 1 : rows + 1] = hidden[:tokens].reshape(rows, width, channels)
        hid[f + 2, jnp.where(low, rows + 1, 0)] = hidden[tokens:]
        hid[f + 2, jnp.where(low, 0, rows + 1)] = jnp.zeros((width, channels), F32)
        attended[f] = result[:tokens]

    def receive(f):
        back_arrival(f, 0).wait_recv()
        result = ret_in[f]
        attended[f] = result
        hid[f + 2, 1 : rows + 1] = activate(result).reshape(rows, width, channels)
        hid[f + 2, jnp.where(low, 0, rows + 1)] = jnp.zeros((width, channels), F32)
        back_arrival(f, 1).wait_recv()

    def settle(f, kept):
        if f > 0:

            @pl.when(sends_past)
            def _():
                past(f, kept).start()

        for r in range(rows + 2):
            place(f + 2, r)

    def prepare():
        for c in local[:-1]:
            c.wait()
        m1 = dot3(split(wq[...]), split(wk[...]), TRANSPOSED) * (1.0 / math.sqrt(channels))
        m1h[...], m1l[...] = split(m1)
        m2h[...], m2l[...] = split(dot3(split(wv[...]), split(wo[...])))

    def follow(order, is_inner):
        waited = set()
        kept = pl.ds(0, rows + 2) if is_inner else pl.ds(jnp.where(low, 1, 0), rows + 1)

        def once(key, wait):
            if key not in waited:
                waited.add(key)
                wait()

        def wait_line(f, slot):
            once((f, slot), lambda: line(f, slot).wait_recv())

        def take_past(f):
            @pl.when(has_past)
            def _():
                past(f, kept, True).wait_recv()
                if not is_inner:
                    hid[f - 1, jnp.where(low, 0, rows + 1)] = jnp.zeros((width, channels), F32)

            @pl.when(jnp.logical_not(has_past))
            def _():
                hid[f - 1] = jnp.zeros(hid.shape[1:], F32)

            for r in range(rows + 2):
                place(f - 1, r)

        def do_conv(first, count, t, times):
            once("own rows", lambda: local[-1].wait())
            for k in range(first, first + count):
                once(("core", k // 3), lambda: core_arrival(2 - k // 3).wait_recv())
                for kind in (2, 3):
                    once((kind, "shard", k), lambda: shard_arrival(kind, k).wait_recv())
            conv(first, count, t, times)

        def turn(f):
            if not is_inner:
                if f < frames - 1:
                    receive(f)
                else:
                    for slot in range(3):
                        gather(slot).wait_recv()
                    attend_outer(f)
            else:
                for slot in (1, 0, 2):
                    wait_line(f, slot)
                attend_inner(f)
            settle(f, kept)

        for name, *at in order:
            if name == "W":
                step(*at)
            elif name == "conv":
                do_conv(*at)
            elif name == "att":
                turn(*at)
            elif name == "past":
                take_past(*at)
            elif name == "pre":
                prepare()
            elif name == "own":
                line(at[0], 1).start()
            elif name == "fwd":
                wait_line(at[0], 0)
                line(at[0], 2).start()
            elif name == "gat":
                if at[0] > 0:
                    wait_line(frames - 1, at[0])
                gather(at[0]).start()

    pl.when(inner)(lambda: follow(INNER_ORDER, True))
    pl.when(outer)(lambda: follow(OUTER_ORDER, False))

    @pl.when(inner)
    def _():
        for f in range(frames):
            line(f, 1).wait_send()
            line(f, 2).wait_send()
            if f + 1 < frames:
                back(f, 0).wait_send()
                back(f, 1).wait_send()
        for slot in range(3):
            gather(slot).wait_send()

    @pl.when(outer)
    def _():
        for f in range(frames):
            line(f, 0).wait_send()

    def leave(kept):
        past(1, kept).wait_send()
        past(2, kept).wait_send()

    pl.when(sends_past)(lambda: each_past(leave))
    for c in core_copies:
        c.wait_send()
    for k in range(BLOCKS):
        for kind in range(6 if k in QUARTERED else 4):
            shard_copy(kind, k).wait_send()


def hand_on(a, b, a_out, b_out):
    a_out[...] = a[...]
    b_out[...] = b[...]


def paired(own, gain_attention, w_query, w_key, w_value, w_out, gain_conv, conv_weight, rows):
    frames, tokens, channels = own.shape
    width = tokens // rows
    taps = conv_weight.shape[0]
    vmem, dma = pltpu.VMEM, pltpu.SemaphoreType.DMA
    results = pl.pallas_call(
        pair_kernel,
        in_specs=[pl.BlockSpec(memory_space=pl.ANY)] * 8,
        out_specs=[pl.BlockSpec(memory_space=pltpu.VMEM)] * 2,
        out_shape=[
            jax.ShapeDtypeStruct(own.shape, F32),
            jax.ShapeDtypeStruct((frames * tokens, channels), F32),
        ],
        scratch_shapes=[
            vmem(own.shape, F32),
            vmem((channels,), F32),
            *[vmem((channels, channels), F32)] * 4,
            vmem((channels,), F32),
            vmem((frames, 3, tokens, channels), F32),
            vmem((frames + 2, rows + 2, width, channels), F32),
            vmem((frames, tokens, channels), F32),
            vmem((frames, tokens, channels), F32),
            vmem((taps, channels, channels), F32),
            *[vmem((channels, channels), BF16)] * 4,
            *[vmem((frames + 2, rows + 2, width, 3 * channels), BF16)] * 2,
            dma((8,)),
            dma((frames, 3)),
            dma((frames, 3)),
            dma((frames, 2)),
            dma((frames, 2)),
            dma((3,)),
            dma((3,)),
            dma((2,)),
            dma((2,)),
            dma((6, BLOCKS)),
            dma((6, BLOCKS)),
            dma((3,)),
            dma((3,)),
        ],
        compiler_params=pltpu.CompilerParams(
            collective_id=0, has_side_effects=True, vmem_limit_bytes=VMEM_LIMIT
        ),
    )(own, gain_attention, w_query, w_key, w_value, w_out, gain_conv, conv_weight)
    return pl.pallas_call(
        hand_on,
        in_specs=[pl.BlockSpec(memory_space=pltpu.VMEM)] * 2,
        out_specs=[pl.BlockSpec(memory_space=pltpu.VMEM)] * 2,
        out_shape=[jax.ShapeDtypeStruct(r.shape, F32) for r in results],
    )(*results)


def body(activations, gain_attention, w_query, w_key, w_value, w_out, gain_conv, conv_weight):
    frames, rows, width, channels = activations.shape
    tokens = rows * width
    own = activations.reshape(frames, tokens, channels)
    times, tiles = lax.axis_size("tm"), lax.axis_size("tile")
    taps, size = conv_weight.shape[:2]
    if (lax.axis_size("groups"), times, tiles) == (2, 4, 4) and (frames, rows, taps) == (3, 2, 27) and size % 32 == 0:
        attended, conv_out = paired(
            own, gain_attention, w_query, w_key, w_value, w_out, gain_conv, conv_weight, rows
        )
        return (attended.reshape(activations.shape), conv_out.reshape(activations.shape))
    plan = shard_plan(times, lax.axis_size("groups") == 2 and size % 16 == 0)
    vmem = pl.BlockSpec(memory_space=pltpu.VMEM)
    dma = pltpu.SemaphoreType.DMA
    attended, conv_out = pl.pallas_call(
        functools.partial(kernel, plan, times, tiles),
        in_specs=[vmem] * 7 + [pl.BlockSpec(memory_space=pl.ANY)],
        out_specs=[vmem, vmem],
        out_shape=[
            jax.ShapeDtypeStruct(own.shape, F32),
            jax.ShapeDtypeStruct((frames * tokens, channels), F32),
        ],
        scratch_shapes=[
            pltpu.VMEM((frames, tiles - 1, tokens, channels), F32),
            pltpu.VMEM((frames, rows, width, channels), F32),
            pltpu.VMEM((frames, width, channels), F32),
            pltpu.VMEM((frames, width, channels), F32),
            pltpu.VMEM((2, rows, width, channels), F32),
            pltpu.VMEM((2, width, channels), F32),
            pltpu.VMEM((2, width, channels), F32),
            pltpu.VMEM((taps, channels, channels), F32),
            pltpu.VMEM((frames + 2, rows + 2, width, 3 * channels), BF16),
            pltpu.VMEM((frames + 2, rows + 2, width, 3 * channels), BF16),
            dma((frames, 2, tiles - 1)),
            dma((frames, tiles - 1)),
            dma((5 * frames,)),
            dma((5 * frames,)),
            dma((CHUNKS, len(plan))),
            dma((CHUNKS, len(plan))),
            dma,
        ],
        compiler_params=pltpu.CompilerParams(
            collective_id=0, has_side_effects=True, vmem_limit_bytes=VMEM_LIMIT
        ),
    )(
        own, gain_attention, w_query, w_key, w_value, w_out, gain_conv, conv_weight
    )
    return (attended.reshape(activations.shape), conv_out.reshape(activations.shape))


def solution(mesh):
    placed = P(("groups", "tm"), "tile", None, None)
    return jax.shard_map(
        body,
        mesh=mesh,
        in_specs=(placed, P(), P(), P(), P(), P(), P(), P(None, "tm", None)),
        out_specs=(placed, placed),
        check_vma=False,
    )
```

```python
import functools
import math

import jax
import jax.numpy as jnp
from jax import lax
from jax.experimental import pallas as pl
from jax.experimental.pallas import tpu as pltpu
from jax.sharding import PartitionSpec as P

F32, BF16 = jnp.float32, jnp.bfloat16
VMEM_LIMIT = 56 * 1024 * 1024
CHUNKS = 3


def split(x):
    high = x.astype(BF16)
    return high, (x - high.astype(F32)).astype(BF16)


def dot3(a, b, dims=(((1,), (0,)), ((), ()))):
    dot = functools.partial(lax.dot_general, dimension_numbers=dims, preferred_element_type=F32)
    (ah, al), (bh, bl) = a, b
    return dot(ah, bh) + (dot(ah, bl) + dot(al, bh))


TRANSPOSED = (((1,), (1,)), ((), ()))


def rms(v, gain):
    return v * lax.rsqrt(jnp.mean(v * v, axis=-1, keepdims=True) + 1e-06) * gain


MESH = pl.DeviceIdType.MESH


def shard_plan(shards, halved):
    plan, held = [], [(0, 0, None)]
    bit = 1
    while 2 * bit < shards:
        bit *= 2
    while bit >= 1 and shards > 1:
        arrived = []
        for mask, part, source in held:
            if halved and bit > 1 and part == 0:
                plan.append(("tm", bit, mask, 1, source))
                plan.append(("groups", 1, mask ^ bit, 1, len(plan) - 1))
                arrived += [(mask ^ bit, 1, len(plan) - 2), (mask ^ bit, 2, len(plan) - 1)]
            else:
                plan.append(("tm", bit, mask, part, source))
                arrived.append((mask ^ bit, part, len(plan) - 1))
        held += arrived
        bit //= 2
    return plan


def kernel(
    plan, times, tiles, act, gain_a, wq, wk, wv, wo, gain_c, kernel_hbm, attended, out,
    others, hid, up, down, past, past_up, past_down, weights, xh, xl,
    line_send, line_recv, edge_send, edge_recv, shard_send, shard_recv, own_sem,
):
    frames, rows, width, channels = hid.shape
    tokens = rows * width
    group, me, tile = lax.axis_index("groups"), lax.axis_index("tm"), lax.axis_index("tile")
    size = kernel_hbm.shape[1]
    half = size // 2

    barrier = pltpu.get_barrier_semaphore()
    friends = [(True, {"groups": 1 - group})]
    bit = 1
    while bit < times:
        friends.append((True, {"tm": me + bit * (1 - 2 * ((me // bit) % 2))}))
        bit *= 2
    for dt, dz in ((0, 1), (1, 0), (1, 1), (1, -1)):
        for sign in (1, -1):
            t, z = me + sign * dt, tile + sign * dz
            inside = (t >= 0) & (t < times) & (z >= 0) & (z < tiles)
            friends.append((inside, {"tm": t, "tile": z}))
    count = 0
    for inside, device in friends:
        if inside is True:
            pl.semaphore_signal(barrier, inc=1, device_id=device, device_id_type=MESH)
            count = count + 1
        else:

            @pl.when(inside)
            def _(device=device):
                pl.semaphore_signal(barrier, inc=1, device_id=device, device_id_type=MESH)

            count = count + inside.astype(jnp.int32)
    pl.semaphore_wait(barrier, count)

    def copy(src, dst, send, recv, device):
        return pltpu.make_async_remote_copy(
            src_ref=src, dst_ref=dst, send_sem=send, recv_sem=recv, device_id=device, device_id_type=MESH
        )

    def line(f, distance, direction):
        slot_here = distance - 1 if direction > 0 else tiles - distance + 1
        slot_there = distance if direction > 0 else tiles - distance
        src = act.at[f] if distance == 1 else others.at[f, slot_here - 1]
        side = 0 if direction > 0 else 1
        return copy(
            src, others.at[f, slot_there - 1], line_send.at[f, side, distance - 1],
            line_recv.at[f, slot_there - 1], {"tile": tile + direction},
        )

    def sends(distance, direction):
        if direction > 0:
            return (tile >= distance - 1) & (tile < tiles - 1)
        return (tile + distance - 1 <= tiles - 1) & (tile > 0)

    def flip(value, bit):
        return value + bit * (1 - 2 * ((value // bit) % 2))

    def flipped(mask):
        value, bit = me, 1
        while bit <= mask:
            if mask & bit:
                value = flip(value, bit)
            bit *= 2
        return value

    def region(ref, chunk, shard, part, swap, local=False):
        first = group if not swap else 1 - group
        start = {0: 0, 1: first * half, 2: (1 - first) * half}[part]
        row = start if local else shard * size + start
        length = size if part == 0 else half
        if not isinstance(row, int):
            row = pl.multiple_of(row, math.gcd(size, length))
        return ref.at[pl.ds(9 * chunk, 9), pl.ds(row, length)]

    def shard_copy(chunk, k):
        axis, bit, mask, part, source = plan[k]
        there = region(weights, chunk, flipped(mask), part, False)
        src = region(kernel_hbm, chunk, 0, part, False, True) if mask == 0 else there
        device = {"tm": flip(me, bit)} if axis == "tm" else {"groups": 1 - group}
        return copy(src, there, shard_send.at[chunk, k], shard_recv.at[chunk, k], device)

    def shard_arrival(chunk, k):
        axis, bit, mask, part, source = plan[k]
        if axis == "tm":
            here, device = region(weights, chunk, flipped(mask ^ bit), part, False), {"tm": flip(me, bit)}
        else:
            here, device = region(weights, chunk, flipped(mask), part, True), {"groups": 1 - group}
        return copy(here, here, shard_send.at[chunk, k], shard_recv.at[chunk, k], device)

    early = [k for k, step in enumerate(plan) if step[4] is None and any(s[4] == k for s in plan)]
    later = [k for k, step in enumerate(plan) if step[4] is not None and any(s[4] == k for s in plan)]

    waited = set()

    def arrive(chunk, k):
        if (chunk, k) in waited:
            return
        waited.add((chunk, k))
        shard_arrival(chunk, k).wait_recv()
        if k in early and chunk + 1 < CHUNKS:
            shard_copy(chunk + 1, k).start()
        for j, step in enumerate(plan):
            if step[4] == k:
                shard_copy(chunk, j).start()

    def start_line(f):
        for direction in (1, -1):

            @pl.when(sends(1, direction))
            def _(direction=direction):
                line(f, 1, direction).start()

    start_line(0)
    for chunk in range(CHUNKS):
        for k, step in enumerate(plan):
            if step[4] is None and (chunk == 0 or k not in early):
                shard_copy(chunk, k).start()
    own_rows = weights.at[:, pl.ds(pl.multiple_of(me * size, size), size)]
    own_copy = pltpu.make_async_copy(kernel_hbm, own_rows, own_sem)
    own_copy.start()

    cell = lax.broadcasted_iota(jnp.int32, (width, channels), 0)

    def place(f, r):
        upper, middle, lower, t = (past_up, past, past_down, f) if f < 2 else (up, hid, down, f - 2)
        value = upper[t] if r == 0 else lower[t] if r == rows + 1 else middle[t, r - 1]
        before = jnp.where(cell == 0, 0.0, pltpu.roll(value, 1, 0))
        after = jnp.where(cell == width - 1, 0.0, pltpu.roll(value, width - 1, 0))
        for c, v in enumerate((before, value, after)):
            high, low = split(v)
            xh[f, r, :, c * channels : (c + 1) * channels] = high
            xl[f, r, :, c * channels : (c + 1) * channels] = low

    gain = gain_a[...].reshape(1, channels)
    scale = 1.0 / math.sqrt(channels)
    edges = []

    def edge(number, src, dst, dt, dz):
        t, z = me + dt, tile + dz
        goes = (t < times) & (z >= 0) & (z < tiles)
        comes = (me - dt >= 0) & (tile - dz >= 0) & (tile - dz < tiles)
        move = copy(src, dst, edge_send.at[number], edge_recv.at[number], {"tm": t, "tile": z})

        @pl.when(goes)
        def _():
            move.start()

        edges.append((goes, comes, move, dst))

    for f in range(frames):
        for distance in range(1, tiles):
            for direction in (1, -1):
                comes = tile >= distance if direction > 0 else tile + distance < tiles

                @pl.when(comes)
                def _(f=f, distance=distance, direction=direction):
                    slot = distance if direction > 0 else tiles - distance
                    here = others.at[f, slot - 1]
                    side = 0 if direction > 0 else 1
                    copy(
                        here, here, line_send.at[f, side, distance - 1], line_recv.at[f, slot - 1],
                        {"tile": tile - direction},
                    ).wait_recv()

                if distance + 1 < tiles:

                    @pl.when(sends(distance + 1, direction))
                    def _(f=f, distance=distance, direction=direction):
                        line(f, distance + 1, direction).start()

            if distance == 1 and f + 1 < frames:
                start_line(f + 1)
        if tiles == 1 and f + 1 < frames:
            start_line(f + 1)
        if f < CHUNKS and f < frames - 1:
            for k in early:
                arrive(f, k)
        x = act[f]
        normed = split(rms(x, gain))
        queries = dot3(normed, split(wq[...]))
        folded = split(dot3(split(queries), split(wk[...]), TRANSPOSED))
        cells = [normed] + [split(rms(others[f, s], gain)) for s in range(tiles - 1)]
        keys = tuple(jnp.concatenate([c[i] for c in cells], axis=0) for i in range(2))
        scores = dot3(folded, keys, TRANSPOSED) * scale
        powers = jnp.exp(scores - jnp.max(scores, axis=-1, keepdims=True))
        summed = jnp.sum(powers, axis=-1, keepdims=True)
        gathered = dot3(split(powers), keys) / summed
        mixed = dot3(split(gathered), split(wv[...]))
        result = x + dot3(split(mixed), split(wo[...]))
        attended[f] = result
        v = rms(result, gain_c[...].reshape(1, channels))
        hid[f] = (v / (1.0 + jnp.exp(-v))).reshape(rows, width, channels)
        base = 5 * f
        edge(base, hid.at[f, rows - 1], up.at[f], 0, 1)
        edge(base + 1, hid.at[f, 0], down.at[f], 0, -1)
        if f >= frames - 2:
            p = f - (frames - 2)
            edge(base + 2, hid.at[f], past.at[p], 1, 0)
            edge(base + 3, hid.at[f, rows - 1], past_up.at[p], 1, 1)
            edge(base + 4, hid.at[f, 0], past_down.at[p], 1, -1)
        for r in range(1, rows + 1):
            place(f + 2, r)
        if 1 <= f < frames - 1 and f <= CHUNKS:
            for k in later:
                arrive(f - 1, k)

    for chunk in range(CHUNKS):
        for k in early:
            arrive(chunk, k)
    for goes, comes, move, dst in edges:

        @pl.when(comes)
        def _(move=move):
            move.wait_recv()

        @pl.when(jnp.logical_not(comes))
        def _(dst=dst):
            dst[...] = jnp.zeros(dst.shape, F32)

    for f in range(frames + 2):
        for r in range(rows + 2):
            if f < 2 or r in (0, rows + 1):
                place(f, r)
    for chunk in range(CHUNKS):
        for k in later:
            arrive(chunk, k)
    own_copy.wait()
    pixels = frames * tokens
    for a in range(CHUNKS):
        for k in range(len(plan)):
            arrive(a, k)

        def row_taps(b, carry, a=a):
            block = weights[pl.ds(9 * a + 3 * b, 3)].reshape(3 * channels, channels)
            high = xh[pl.ds(a, frames), pl.ds(b, rows)].reshape(pixels, 3 * channels)
            low = xl[pl.ds(a, frames), pl.ds(b, rows)].reshape(pixels, 3 * channels)
            product = dot3((high, low), split(block))
            out[...] = out[...] + product
            return carry

        if a == 0:
            out[...] = jnp.zeros(out.shape, F32)
        lax.fori_loop(0, 3, row_taps, 0)

    for f in range(frames):
        for distance in range(1, tiles):
            for direction in (1, -1):

                @pl.when(sends(distance, direction))
                def _(f=f, distance=distance, direction=direction):
                    line(f, distance, direction).wait_send()

    for goes, comes, move, dst in edges:

        @pl.when(goes)
        def _(move=move):
            move.wait_send()

    for chunk in range(CHUNKS):
        for k in range(len(plan)):
            shard_copy(chunk, k).wait_send()


PIECES = (
    (0, 0, 1), (0, 1, 2), (1, 0, 3), (2, 0, 3), (3, 0, 3), (4, 0, 3), (5, 0, 3), (6, 0, 3), (7, 0, 3),
    (8, 0, 2), (8, 2, 1),
)
AHEAD, QUARTERED = 10, (0, 1, 2, 7)
INNER_ORDER = (
    ("gat", 0), ("W", 0, 0), ("fwd", 0), ("W", 1, 0), ("own", 1), ("W", 2, 0), ("pre",), ("fwd", 1), ("W", 0, 1),
    ("ata", 0), ("W", 1, 1), ("W", 3, 0), ("own", 2), ("W", 2, 1), ("att", 0), ("W", 0, 2), ("W", 4, 0), ("ata", 1),
    ("W", 3, 1), ("att", 1), ("W", 5, 0), ("fwd", 2), ("W", 0, 3), ("W", 1, 2), ("ata", 2), ("W", 1, 3),
    ("W", 6, 0), ("gat", 1), ("W", 4, 1), ("W", 2, 2), ("gat", 2), ("W", 7, 0), ("att", 2), ("W", 5, 1),
    ("W", 2, 3), ("W", 8, 0), ("conv", 2, 4, 1, 1), ("conv", 0, 4, 1, 1), ("W", 6, 1), ("conv", 0, 2, 2, 1),
    ("W", 7, 1), ("conv", 1, 4, 1, 1), ("conv", 3, 2, 2, 1), ("W", 9, 0), ("conv", 1, 2, 2, 1), ("W", 7, 2),
    ("W", 10, 0), ("conv", 4, 2, 2, 1), ("conv", 2, 2, 2, 1), ("W", 8, 1), ("past", 1), ("conv", 5, 2, 2, 1),
    ("W", 9, 1), ("W", 7, 3), ("past", 2), ("W", 10, 1), ("conv", 3, 1, 1, 3), ("conv", 6, 0, 3, 3),
)
OUTER_ORDER = (
    ("pre",), ("W", 0, 0), ("W", 0, 1), ("W", 1, 0), ("W", 0, 2), ("W", 1, 1), ("W", 2, 0), ("W", 1, 2),
    ("W", 3, 0), ("W", 2, 1), ("W", 4, 0), ("W", 2, 2), ("W", 5, 0), ("W", 3, 1), ("W", 6, 0), ("W", 0, 3),
    ("W", 1, 3), ("W", 4, 1), ("att", 0), ("W", 5, 1), ("W", 7, 0), ("W", 2, 3), ("conv", 0, 2, 1, 3), ("att", 1),
    ("W", 8, 0), ("ata", 2), ("W", 6, 1), ("W", 7, 1), ("conv", 3, 2, 2, 3), ("W", 9, 0), ("W", 10, 0), ("att", 2),
    ("W", 8, 1), ("W", 7, 2), ("conv", 0, 3, 2, 3), ("W", 7, 3), ("W", 9, 1), ("past", 1), ("W", 10, 1),
    ("past", 2), ("conv", 3, 1, 1, 3), ("conv", 6, 0, 3, 3),
)


def first_tap(k):
    return 9 * (2 - k // 3) + 3 * (k % 3)


def pair_kernel(
    act_hbm, gain_a_hbm, wq_hbm, wk_hbm, wv_hbm, wo_hbm, gain_c_hbm, kernel_hbm, attended_hbm, out_hbm,
    attended, out, act, gain_a, wq, wk, wv, wo, gain_c, others, hid, ret, ret_in, weights, m1h, m1l, m2h, m2l, kh, kl, fh, fl, xh, xl,
    local_sem, out_sem, line_send, line_recv, ret_send, ret_recv, gather_send, gather_recv, past_send, past_recv, shard_send, shard_recv, core_send, core_recv,
):
    frames, tokens, channels = act.shape
    width = hid.shape[2]
    rows = tokens // width
    group, me, tile = lax.axis_index("groups"), lax.axis_index("tm"), lax.axis_index("tile")
    size = kernel_hbm.shape[1]
    half, quarter = size // 2, size // 4
    inner = (tile == 1) | (tile == 2)
    outer = jnp.logical_not(inner)
    low = tile < 2
    place_in_pair = inner.astype(jnp.int32)
    core_of = me % 2
    side = (me // 2) % 2
    x_partner = {"groups": 1 - group}
    y_partner = {"tm": me + 2 - 4 * side}
    core_partner = {"tm": me + 1 - 2 * core_of}
    pair_partner = {"tile": tile + 1 - 2 * (tile % 2)}
    peer = {"tile": 3 - tile}
    later = {"tm": me + 1}
    sends_past, has_past = me < 3, me > 0

    locals_in = [(act_hbm, act), (gain_a_hbm, gain_a), (wq_hbm, wq), (wk_hbm, wk), (wv_hbm, wv), (wo_hbm, wo), (gain_c_hbm, gain_c)]
    local = [pltpu.make_async_copy(src, dst, local_sem.at[i]) for i, (src, dst) in enumerate(locals_in)]
    own_rows = weights.at[:, pl.ds(pl.multiple_of(me * size, size), size)]
    local.append(pltpu.make_async_copy(kernel_hbm, own_rows, local_sem.at[len(locals_in)]))
    for c in local:
        c.start()

    barrier = pltpu.get_barrier_semaphore()

    def greet(device):
        pl.semaphore_signal(barrier, inc=1, device_id=device, device_id_type=MESH)

    for device in (x_partner, y_partner, core_partner, pair_partner):
        greet(device)
    pl.when(inner)(lambda: greet(peer))
    crossing = me == 1, me == 2
    pl.when(crossing[0])(lambda: greet({"tm": me + 1}))
    pl.when(crossing[1])(lambda: greet({"tm": me - 1}))
    pl.semaphore_wait(barrier, 4 + inner.astype(jnp.int32) + (crossing[0] | crossing[1]).astype(jnp.int32))

    def copy(src, dst, send, recv, device):
        return pltpu.make_async_remote_copy(
            src_ref=src, dst_ref=dst, send_sem=send, recv_sem=recv, device_id=device, device_id_type=MESH
        )

    def line(f, slot):
        src = others.at[f, 0] if slot == 2 else act_hbm.at[f]
        return copy(src, others.at[f, slot], line_send.at[f, slot], line_recv.at[f, slot], pair_partner if slot == 0 else peer)

    def back(f, part):
        if part == 0:
            return copy(ret.at[f], ret_in.at[f], ret_send.at[f, 0], ret_recv.at[f, 0], pair_partner)
        near, far = jnp.where(low, 1, rows), jnp.where(low, rows + 1, 0)
        return copy(hid.at[f + 2, near], hid.at[f + 2, far], ret_send.at[f, 1], ret_recv.at[f, 1], pair_partner)

    def back_arrival(f, part):
        if part == 0:
            return copy(ret_in.at[f], ret_in.at[f], ret_send.at[f, 0], ret_recv.at[f, 0], pair_partner)
        here = hid.at[f + 2, jnp.where(low, rows + 1, 0)]
        return copy(here, here, ret_send.at[f, 1], ret_recv.at[f, 1], pair_partner)

    def gather(slot):
        src = act_hbm.at[frames - 1] if slot == 0 else others.at[frames - 1, slot]
        return copy(src, others.at[frames - 1, slot], gather_send.at[slot], gather_recv.at[slot], pair_partner)

    def past(f, kept, arriving=False):
        there = hid.at[(f - 1, kept)]
        src = there if arriving else hid.at[(f + 2, kept)]
        return copy(src, there, past_send.at[f - 1], past_recv.at[f - 1], later)

    def each_past(act_on):
        pl.when(inner)(lambda: act_on(pl.ds(0, rows + 2)))
        pl.when(outer)(lambda: act_on(pl.ds(jnp.where(low, 1, 0), rows + 1)))

    def taps_of(k):
        block, tap, taps = PIECES[k]
        return pl.ds(first_tap(block) + tap, taps)

    def region(ref, k, shard, which, where):
        row = which * half
        length = half
        if where is not None:
            row, length = row + where * quarter, quarter
        if shard is not None:
            row = row + shard * size
        return ref.at[taps_of(k), pl.ds(pl.multiple_of(row, quarter), length)]

    foreign, theirs = me + 2 - 4 * side, me + 1 - 2 * core_of
    there = theirs + 2 - 4 * side

    def shard_copy(kind, k):
        q = place_in_pair if k in QUARTERED else None
        sems = shard_send.at[kind, k], shard_recv.at[kind, k]
        if kind == 0:
            return copy(region(kernel_hbm, k, None, group, q), region(weights, k, me, group, q), *sems, y_partner)
        if kind == 1:
            ref = region(weights, k, foreign, group, q)
            return copy(ref, ref, *sems, x_partner)
        if kind in (2, 3):
            ref = region(weights, k, foreign, group if kind == 2 else 1 - group, None)
            return copy(ref, ref, *sems, core_partner)
        ref = region(weights, k, foreign, group if kind == 4 else 1 - group, q)
        return copy(ref, ref, *sems, pair_partner)

    def shard_arrival(kind, k):
        q = place_in_pair if k in QUARTERED else None
        sems = shard_send.at[kind, k], shard_recv.at[kind, k]
        if kind == 0:
            ref, device = region(weights, k, foreign, group, q), y_partner
        elif kind == 1:
            ref, device = region(weights, k, foreign, 1 - group, q), x_partner
        elif kind in (2, 3):
            ref, device = region(weights, k, there, group if kind == 2 else 1 - group, None), core_partner
        else:
            ref, device = region(weights, k, foreign, group if kind == 4 else 1 - group, 1 - q), pair_partner
        return copy(ref, ref, *sems, device)

    def send(kind, k):
        shard_copy(kind, k).start()

    def step(k, stage):
        quartered = k in QUARTERED
        if stage == 0:
            shard_arrival(0, k).wait_recv()
            if k + AHEAD < len(PIECES):
                send(0, k + AHEAD)
            send(1, k)
            send(4 if quartered else 2, k)
        elif stage == 1:
            shard_arrival(1, k).wait_recv()
            send(5 if quartered else 3, k)
        elif quartered:
            shard_arrival(4 if stage == 2 else 5, k).wait_recv()
            send(stage, k)

    core_copies = [
        copy(
            kernel_hbm.at[pl.ds(9 * a, 9)], weights.at[pl.ds(9 * a, 9), pl.ds(pl.multiple_of(me * size, size), size)],
            core_send.at[a], core_recv.at[a], core_partner,
        )
        for a in (2, 1, 0)
    ]

    def core_arrival(a):
        ref = weights.at[pl.ds(9 * a, 9), pl.ds(pl.multiple_of(theirs * size, size), size)]
        return copy(ref, ref, core_send.at[a], core_recv.at[a], core_partner)

    def conv(first, t, times, merged):
        a, b = 2 - first // 3, first % 3

        def rows_of(x):
            parts = [x[t : t + times, b + i : b + i + rows].reshape(times * tokens, 3 * channels) for i in range(merged)]
            return parts[0] if merged == 1 else jnp.concatenate(parts, axis=1)

        block = weights[9 * a + 3 * b : 9 * a + 3 * (b + merged)].reshape(merged * 3 * channels, channels)
        high, low_part = split(block)
        both = jnp.dot(rows_of(xh), jnp.concatenate([high, low_part], axis=1), preferred_element_type=F32)
        rest = jnp.dot(rows_of(xl), high, preferred_element_type=F32)
        here = slice((t - a) * tokens, (t - a + times) * tokens)
        out[here] = out[here] + (both[:, :channels] + (both[:, channels:] + rest))

    @pl.when(inner)
    def _():
        line(0, 1).start()

    @pl.when(outer)
    def _():
        for f in range(frames):
            line(f, 0).start()

    for k in range(AHEAD):
        send(0, k)
    for c in core_copies:
        c.start()
    out[...] = jnp.zeros(out.shape, F32)

    cell = lax.broadcasted_iota(jnp.int32, (width, channels), 0)

    def place(t, r):
        value = hid[t, r]
        before = jnp.where(cell == 0, 0.0, pltpu.roll(value, 1, 0))
        after = jnp.where(cell == width - 1, 0.0, pltpu.roll(value, width - 1, 0))
        for c, v in enumerate((before, value, after)):
            xh[t, r, :, c * channels : (c + 1) * channels], xl[t, r, :, c * channels : (c + 1) * channels] = split(v)

    def activate(v):
        v = rms(v, gain_c[...].reshape(1, channels))
        return v / (1.0 + jnp.exp(-v))

    def add_keys(first, tiles):
        for i, v in enumerate(tiles):
            here = slice((first + i) * tokens, (first + i + 1) * tokens)
            kh[here], kl[here] = split(rms(v, gain_a[...].reshape(1, channels)))

    def fold(asked):
        normed = split(rms(asked, gain_a[...].reshape(1, channels)))
        fh[: asked.shape[0]], fl[: asked.shape[0]] = split(dot3(normed, (m1h[...], m1l[...])))

    def attend(asked):
        keys = kh[...], kl[...]
        scores = dot3((fh[: asked.shape[0]], fl[: asked.shape[0]]), keys, TRANSPOSED)
        powers = jnp.exp(scores - jnp.max(scores, axis=-1, keepdims=True))
        summed = jnp.sum(powers, axis=-1, keepdims=True)
        gathered = dot3(split(powers), keys) / summed
        return asked + dot3(split(gathered), (m2h[...], m2l[...]))

    def row_of(f, slot, first):
        return others[f, slot, pl.ds(pl.multiple_of(jnp.where(first, 0, tokens - width), width), width)]

    def asked_by(f, is_inner):
        if not is_inner:
            return jnp.concatenate([act[f], row_of(f, 0, low)], axis=0)
        partner = row_of(f, 0, jnp.logical_not(low)) if f == frames - 1 else others[f, 0]
        return jnp.concatenate([act[f], partner, row_of(f, 1, low)], axis=0)

    def attend_inner(f):
        last = f == frames - 1
        add_keys(3, (others[f, 2],))
        result = attend(asked_by(f, True))
        if not last:
            ret[f] = result[tokens : 2 * tokens]
            back(f, 0).start()
        hidden = activate(result)
        hid[f + 2, 1 : rows + 1] = hidden[:tokens].reshape(rows, width, channels)
        if not last:
            back(f, 1).start()
        attended[f] = result[:tokens]
        edge = hidden[tokens : tokens + width]
        if not last:
            edge = jnp.where(low, hidden[2 * tokens - width : 2 * tokens], edge)
        beyond = hidden[-width:]
        hid[f + 2, 0] = jnp.where(low, edge, beyond)
        hid[f + 2, rows + 1] = jnp.where(low, beyond, edge)

    def attend_outer(f):
        add_keys(2, (others[f, 1], others[f, 2]))
        result = attend(asked_by(f, False))
        hidden = activate(result)
        hid[f + 2, 1 : rows + 1] = hidden[:tokens].reshape(rows, width, channels)
        hid[f + 2, jnp.where(low, rows + 1, 0)] = hidden[tokens:]
        hid[f + 2, jnp.where(low, 0, rows + 1)] = jnp.zeros((width, channels), F32)
        attended[f] = result[:tokens]

    def receive(f):
        back_arrival(f, 0).wait_recv()
        result = ret_in[f]
        attended[f] = result
        hid[f + 2, 1 : rows + 1] = activate(result).reshape(rows, width, channels)
        hid[f + 2, jnp.where(low, 0, rows + 1)] = jnp.zeros((width, channels), F32)
        back_arrival(f, 1).wait_recv()

    def store(f):
        return pltpu.make_async_copy(attended.at[f], attended_hbm.at[f], out_sem.at[f])

    def settle(f, kept):
        store(f).start()
        if f > 0:

            @pl.when(sends_past)
            def _():
                past(f, kept).start()

        for r in range(rows + 2):
            place(f + 2, r)

    def prepare():
        for c in local[:-1]:
            c.wait()
        m1 = dot3(split(wq[...]), split(wk[...]), TRANSPOSED) * (1.0 / math.sqrt(channels))
        m1h[...], m1l[...] = split(m1)
        m2h[...], m2l[...] = split(dot3(split(wv[...]), split(wo[...])))

    def follow(order, is_inner):
        waited = set()
        kept = pl.ds(0, rows + 2) if is_inner else pl.ds(jnp.where(low, 1, 0), rows + 1)

        def once(key, wait):
            if key not in waited:
                waited.add(key)
                wait()

        def wait_line(f, slot):
            once((f, slot), lambda: line(f, slot).wait_recv())

        def take_past(f):
            @pl.when(has_past)
            def _():
                past(f, kept, True).wait_recv()
                if not is_inner:
                    hid[f - 1, jnp.where(low, 0, rows + 1)] = jnp.zeros((width, channels), F32)

            @pl.when(jnp.logical_not(has_past))
            def _():
                hid[f - 1] = jnp.zeros(hid.shape[1:], F32)

            for r in range(rows + 2):
                place(f - 1, r)

        def do_conv(first, t, times, merged):
            once("own rows", lambda: local[-1].wait())
            for k in range(first, first + merged):
                once(("core", k // 3), lambda: core_arrival(2 - k // 3).wait_recv())
                for i in [i for i, piece in enumerate(PIECES) if piece[0] == k]:
                    for kind in (2, 3):
                        once((kind, "piece", i), lambda: shard_arrival(kind, i).wait_recv())
            conv(first, t, times, merged)

        def turn(f):
            if not is_inner:
                if f < frames - 1:
                    receive(f)
                else:
                    for slot in (1, 2):
                        gather(slot).wait_recv()
                    attend_outer(f)
            else:
                wait_line(f, 2)
                attend_inner(f)
            settle(f, kept)

        def begin(f):
            if is_inner:
                wait_line(f, 1)
                wait_line(f, 0)
                add_keys(0, (act[f], others[f, 0], others[f, 1]))
            else:
                gather(0).wait_recv()
                add_keys(0, (act[f], others[f, 0]))
            fold(asked_by(f, is_inner))

        for name, *at in order:
            if name == "ata":
                begin(*at)
            elif name == "W":
                step(*at)
            elif name == "conv":
                do_conv(*at)
            elif name == "att":
                turn(*at)
            elif name == "past":
                take_past(*at)
            elif name == "pre":
                prepare()
            elif name == "own":
                line(at[0], 1).start()
            elif name == "fwd":
                wait_line(at[0], 0)
                line(at[0], 2).start()
            elif name == "gat":
                if at[0] > 0:
                    wait_line(frames - 1, at[0])
                gather(at[0]).start()

    pl.when(inner)(lambda: follow(INNER_ORDER, True))
    pl.when(outer)(lambda: follow(OUTER_ORDER, False))
    result_copy = pltpu.make_async_copy(out, out_hbm, out_sem.at[frames])
    result_copy.start()

    @pl.when(inner)
    def _():
        for f in range(frames):
            line(f, 1).wait_send()
            line(f, 2).wait_send()
            if f + 1 < frames:
                back(f, 0).wait_send()
                back(f, 1).wait_send()
        for slot in range(3):
            gather(slot).wait_send()

    @pl.when(outer)
    def _():
        for f in range(frames):
            line(f, 0).wait_send()

    def leave(kept):
        past(1, kept).wait_send()
        past(2, kept).wait_send()

    pl.when(sends_past)(lambda: each_past(leave))
    for c in core_copies:
        c.wait_send()
    for f in range(frames):
        store(f).wait()
    result_copy.wait()
    for k in range(len(PIECES)):
        for kind in range(6 if k in QUARTERED else 4):
            shard_copy(kind, k).wait_send()


def hand_on(a, b, a_out, b_out, a_here, b_here, in_sem, out_sem):
    count = a.shape[0]
    size = b.shape[0] // count
    moves = []
    for i in range(count):
        for n, (src, here, dst) in enumerate(((a, a_here, a_out), (b, b_here, b_out))):
            at = i if n == 0 else slice(i * size, (i + 1) * size)
            moves.append((
                pltpu.make_async_copy(src.at[at], here.at[at], in_sem.at[n, i]),
                pltpu.make_async_copy(here.at[at], dst.at[at], out_sem.at[n, i]),
            ))
    for arrive, _ in moves:
        arrive.start()
    for arrive, leave in moves:
        arrive.wait()
        leave.start()
    for _, leave in moves:
        leave.wait()


def paired(own, gain_attention, w_query, w_key, w_value, w_out, gain_conv, conv_weight, rows):
    frames, tokens, channels = own.shape
    width = tokens // rows
    taps = conv_weight.shape[0]
    vmem, dma = pltpu.VMEM, pltpu.SemaphoreType.DMA
    results = pl.pallas_call(
        pair_kernel,
        in_specs=[pl.BlockSpec(memory_space=pl.ANY)] * 8,
        out_specs=[pl.BlockSpec(memory_space=pl.ANY)] * 2,
        out_shape=[
            jax.ShapeDtypeStruct(own.shape, F32),
            jax.ShapeDtypeStruct((frames * tokens, channels), F32),
        ],
        scratch_shapes=[
            vmem(own.shape, F32),
            vmem((frames * tokens, channels), F32),
            vmem(own.shape, F32),
            vmem((channels,), F32),
            *[vmem((channels, channels), F32)] * 4,
            vmem((channels,), F32),
            vmem((frames, 3, tokens, channels), F32),
            vmem((frames + 2, rows + 2, width, channels), F32),
            vmem((frames, tokens, channels), F32),
            vmem((frames, tokens, channels), F32),
            vmem((taps, channels, channels), F32),
            *[vmem((channels, channels), BF16)] * 4,
            *[vmem((4 * tokens, channels), BF16)] * 2,
            *[vmem((2 * tokens + width, channels), BF16)] * 2,
            *[vmem((frames + 2, rows + 2, width, 3 * channels), BF16)] * 2,
            dma((8,)),
            dma((frames + 1,)),
            dma((frames, 3)),
            dma((frames, 3)),
            dma((frames, 2)),
            dma((frames, 2)),
            dma((3,)),
            dma((3,)),
            dma((2,)),
            dma((2,)),
            dma((6, len(PIECES))),
            dma((6, len(PIECES))),
            dma((3,)),
            dma((3,)),
        ],
        compiler_params=pltpu.CompilerParams(
            collective_id=0, has_side_effects=True, vmem_limit_bytes=VMEM_LIMIT
        ),
    )(own, gain_attention, w_query, w_key, w_value, w_out, gain_conv, conv_weight)
    return pl.pallas_call(
        hand_on,
        in_specs=[pl.BlockSpec(memory_space=pl.ANY)] * 2,
        out_specs=[pl.BlockSpec(memory_space=pl.ANY)] * 2,
        out_shape=[jax.ShapeDtypeStruct(r.shape, F32) for r in results],
        scratch_shapes=[*[vmem(r.shape, F32) for r in results], dma((2, frames)), dma((2, frames))],
    )(*results)


def body(activations, gain_attention, w_query, w_key, w_value, w_out, gain_conv, conv_weight):
    frames, rows, width, channels = activations.shape
    tokens = rows * width
    own = activations.reshape(frames, tokens, channels)
    times, tiles = lax.axis_size("tm"), lax.axis_size("tile")
    taps, size = conv_weight.shape[:2]
    if (lax.axis_size("groups"), times, tiles) == (2, 4, 4) and (frames, rows, taps) == (3, 2, 27) and size % 32 == 0:
        attended, conv_out = paired(
            own, gain_attention, w_query, w_key, w_value, w_out, gain_conv, conv_weight, rows
        )
        return (attended.reshape(activations.shape), conv_out.reshape(activations.shape))
    plan = shard_plan(times, lax.axis_size("groups") == 2 and size % 16 == 0)
    vmem = pl.BlockSpec(memory_space=pltpu.VMEM)
    dma = pltpu.SemaphoreType.DMA
    attended, conv_out = pl.pallas_call(
        functools.partial(kernel, plan, times, tiles),
        in_specs=[vmem] * 7 + [pl.BlockSpec(memory_space=pl.ANY)],
        out_specs=[vmem, vmem],
        out_shape=[
            jax.ShapeDtypeStruct(own.shape, F32),
            jax.ShapeDtypeStruct((frames * tokens, channels), F32),
        ],
        scratch_shapes=[
            pltpu.VMEM((frames, tiles - 1, tokens, channels), F32),
            pltpu.VMEM((frames, rows, width, channels), F32),
            pltpu.VMEM((frames, width, channels), F32),
            pltpu.VMEM((frames, width, channels), F32),
            pltpu.VMEM((2, rows, width, channels), F32),
            pltpu.VMEM((2, width, channels), F32),
            pltpu.VMEM((2, width, channels), F32),
            pltpu.VMEM((taps, channels, channels), F32),
            pltpu.VMEM((frames + 2, rows + 2, width, 3 * channels), BF16),
            pltpu.VMEM((frames + 2, rows + 2, width, 3 * channels), BF16),
            dma((frames, 2, tiles - 1)),
            dma((frames, tiles - 1)),
            dma((5 * frames,)),
            dma((5 * frames,)),
            dma((CHUNKS, len(plan))),
            dma((CHUNKS, len(plan))),
            dma,
        ],
        compiler_params=pltpu.CompilerParams(
            collective_id=0, has_side_effects=True, vmem_limit_bytes=VMEM_LIMIT
        ),
    )(
        own, gain_attention, w_query, w_key, w_value, w_out, gain_conv, conv_weight
    )
    return (attended.reshape(activations.shape), conv_out.reshape(activations.shape))


def solution(mesh):
    placed = P(("groups", "tm"), "tile", None, None)
    return jax.shard_map(
        body,
        mesh=mesh,
        in_specs=(placed, P(), P(), P(), P(), P(), P(), P(None, "tm", None)),
        out_specs=(placed, placed),
        check_vma=False,
    )
```
